512 devices in a mesh: gx: 32 (over z, y_lo), gy: 16 (over y_hi, x, core).
Axes of the slice: x: 4, y: 4 (y_hi: 2, y_lo: 2; y = y_hi * 2 + y_lo), z: 16, core: 2. Of those that a mesh axis runs over, the one named last changes fastest.
Arguments:
- delta: float32 [4, 512, 256, 128], P(None, 'gx', 'gy'), may hold values from -6 to 6
- alpha: float32 [32, 64, 4, 128], P('gx', 'gy'), may hold values from -6 to 6
- eddy: float32 [512, 256, 128], P('gx', 'gy'), may hold values from 0.02 to 0.2
- courant: float32 [2, 512, 256, 128], P(None, 'gx', 'gy'), may hold values from -0.4 to 0.4
- tile_map: int32 [512, 256], P('gx', 'gy'), may hold values from 0 to 63
- obs_rows: float32 [4096, 3, 128], P(('gx', 'gy')), may hold values from -6 to 6
- gate_beam: int32 [32, 16, 256], P('gx', 'gy'), may hold values from 0 to 255
- gate_index: int32 [32, 16, 256], P('gx', 'gy'), may hold values from 0 to 127
- gate_column: int32 [32, 16, 256], P('gx', 'gy'), may hold values from 0 to 255
- gate_live: int32 [32, 16, 256], P('gx', 'gy'), may hold values 0 or 1
- obs_weight: float32 [32, 16, 256, 4, 128], P('gx', 'gy'), may hold values from -0.25 to 0.25
- obs_precision: float32 [32, 16, 256], P('gx', 'gy'), may hold values from 4 to 64
Outputs:
- grad_delta: float32 [4, 512, 256, 128], P(None, 'gx', 'gy')
- grad_alpha: float32 [32, 64, 4, 128], P('gx', 'gy')
The draws below stay inside these ranges and needn't reach their ends.
Inputs may be any that keep to these rules, and one draw needn't show every extreme that they name: `gate_beam`: a slot's beam is numbered within its own north-south row of tiles as the east-west index of the beam's owner times 8 plus its place among that owner's beams. `gate_column`: column index within the tile is east-west offset times 16 plus north-south offset.
All inputs are finite; a program needn't handle non-finite values. No bound on the sum of `gate_live` on one device may be relied on, other than what follows from the above.
Results may differ from the reference program's by a relative error of at most 0.00011.
Values sent between devices are 32-bit elements; how exact they have to be, the bound alone decides.
A program may use at most 64 MiB of HBM per device.

```python
import math
import jax
import jax.numpy as jnp
from jax import lax

CX = 16
CY = 16
NZ = 128
STEPS = 3
BD = 8
NG = 128
GT = 256
NX = 512
NY = 256
NCT = 64
BEAMS = 4096
N_GX = 32
N_GY = 16


def touch_ends(drawn, key, smallest, largest):
    place = [jax.random.randint(jax.random.fold_in(key, axis), (), 0, length) for axis, length in enumerate(drawn.shape)]
    longest = drawn.shape.index(max(drawn.shape))
    next_to = place[:longest] + [(place[longest] + 1) % drawn.shape[longest]] + place[longest + 1:]
    return drawn.at[tuple(place)].set(smallest).at[tuple(next_to)].set(largest)


def steps_of(key, shape, pieces, least, top_value):
    gain = 1.0
    for dim, blocks in pieces:
        draws = jax.random.uniform(jax.random.fold_in(jax.random.fold_in(key, 6), dim), (blocks,), jnp.float32, least / len(pieces), top_value / len(pieces))
        gain = gain * jnp.repeat(jnp.exp(draws), shape[dim] // blocks).reshape((-1,) + (1,) * (len(shape) - 1 - dim))
    return gain


def normal_values(rng, dims, scale, most, shards=(), held_as=jnp.bfloat16):
    array = jax.random.normal(rng, dims, jnp.float32) * scale
    if len(shards) > 0:
        array = steps_of(rng, dims, shards, -0.22, 0.18) * array
    return jnp.clip(array, min=-most, max=most).astype(held_as)


def setup_inputs(seed: int = 0) -> dict:
    streams_of = jax.random.split(jax.random.key(seed), 13)
    delta = normal_values(streams_of[0], (4, NX, NY, NZ), 1.0, 6.0, ((1, 32), (2, 16)), jnp.float32)
    alpha = normal_values(streams_of[1], (N_GX, NCT, 4, NZ), 1.0, 6.0, ((0, 32), (1, 16)), jnp.float32)
    eddy = jnp.clip(jnp.exp(math.log(0.2) - 2.3025851 * jax.random.uniform(streams_of[2], (NX, NY, NZ), jnp.float32) ** steps_of(streams_of[2], (NX, NY, NZ), ((0, 32), (1, 16)), -0.2, 0.2)), 0.02, 0.2)
    courant = jnp.clip(jax.random.uniform(streams_of[3], (2, NX, NY, NZ), jnp.float32, -0.4, 0.4) * steps_of(streams_of[3], (2, NX, NY, NZ), ((1, 32), (2, 16)), -0.4, 0.0), -0.4, 0.4)
    tile_map = touch_ends(jax.random.randint(streams_of[4], (NX, NY), 0, NCT), jax.random.fold_in(streams_of[4], 1), 0, NCT - 1).astype(jnp.int32)
    obs_rows = normal_values(streams_of[5], (BEAMS, STEPS, NG), 1.0, 6.0, ((0, 512),), jnp.float32)
    gate_beam = touch_ends(jax.random.randint(streams_of[6], (N_GX, N_GY, GT), 0, N_GX * BD), jax.random.fold_in(streams_of[6], 1), 0, (N_GX * BD) - 1).astype(jnp.int32)
    gate_index = touch_ends(jax.random.randint(streams_of[7], (N_GX, N_GY, GT), 0, NG), jax.random.fold_in(streams_of[7], 1), 0, NG - 1).astype(jnp.int32)
    gate_column = touch_ends(jax.random.randint(streams_of[8], (N_GX, N_GY, GT), 0, CX * CY), jax.random.fold_in(streams_of[8], 1), 0, (CX * CY) - 1).astype(jnp.int32)
    gate_live = touch_ends((jax.random.randint(streams_of[9], (N_GX, N_GY, GT), 0, 4) < 3).astype(jnp.int32), jax.random.fold_in(streams_of[9], 1), 0, 1)
    obs_weight = normal_values(streams_of[10], (N_GX, N_GY, GT, 4, NZ), (4 * NZ) ** -0.5, 0.25, ((0, 32), (1, 16)), jnp.float32)
    obs_precision = jnp.clip(jnp.exp(math.log(64.0) - 2.7725887 * jax.random.uniform(streams_of[11], (N_GX, N_GY, GT), jnp.float32) ** steps_of(streams_of[11], (N_GX, N_GY, GT), ((0, 32), (1, 16)), -0.2, 0.2)), 4.0, 64.0)
    return {"delta": delta, "alpha": alpha, "eddy": eddy, "courant": courant, "tile_map": tile_map, "obs_rows": obs_rows, "gate_beam": gate_beam, "gate_index": gate_index, "gate_column": gate_column, "gate_live": gate_live, "obs_weight": obs_weight, "obs_precision": obs_precision}


profile_weight = 0.125
highest = lax.Precision.HIGHEST

def advance(state, eddy, courant):
    padded = jnp.pad(state, ((0, 0), (1, 1), (1, 1), (0, 0)))
    east_side = padded[:, 2:, 1:-1]
    west_side = padded[:, :-2, 1:-1]
    north_side = padded[:, 1:-1, 2:]
    south_side = padded[:, 1:-1, :-2]
    return state + eddy * (east_side + west_side + north_side + south_side - 4.0 * state) - 0.5 * courant[0] * (east_side - west_side) - 0.5 * courant[1] * (north_side - south_side)

def to_tiles(grid):
    return grid.reshape(4, N_GX, CX, N_GY, CY, NZ).transpose(1, 3, 0, 2, 4, 5).reshape(N_GX, N_GY, 4, CX * CY, NZ)

def from_tiles(tiles):
    return tiles.reshape(N_GX, N_GY, 4, CX, CY, NZ).transpose(2, 0, 3, 1, 4, 5).reshape(4, NX, NY, NZ)

def tile_seen(tile, columns, weights):
    picked = jnp.take(tile, columns, axis=1)
    return jnp.einsum('cgz,gcz->g', picked, weights, precision=highest)

def tile_push(misfit, columns, weights):
    pushed = jax.ops.segment_sum(misfit[:, None, None] * weights, columns, num_segments=CX * CY)
    return jnp.transpose(pushed, (1, 0, 2))

def reference(delta, alpha, eddy, courant, tile_map, obs_rows, gate_beam, gate_index, gate_column, gate_live, obs_weight, obs_precision):
    column_x = (jnp.arange(NX, dtype=jnp.int32) // CX)[:, None]
    profiles = alpha[column_x, tile_map]
    state = delta + profile_weight * jnp.transpose(profiles, (2, 0, 1, 3))
    row_y = jnp.arange(N_GY, dtype=jnp.int32)[None, :, None]
    owner_beam = (gate_beam // BD * N_GY + row_y) * BD + gate_beam % BD
    scaled = gate_live.astype(jnp.float32) * obs_precision
    seen_fn = jax.vmap(jax.vmap(tile_seen))
    push_fn = jax.vmap(jax.vmap(tile_push))
    forcings = []
    for step in range(STEPS):
        state = advance(state, eddy, courant)
        seen = seen_fn(to_tiles(state), gate_column, obs_weight)
        observed = obs_rows[owner_beam, step, gate_index]
        misfit = scaled * (seen - observed)
        forcings.append(from_tiles(push_fn(misfit, gate_column, obs_weight)))
    adjoint = forcings[STEPS - 1]
    for step in range(STEPS - 1, -1, -1):
        _, backward = jax.vjp(lambda value: advance(value, eddy, courant), adjoint)
        adjoint = backward(adjoint)[0]
        if step > 0:
            adjoint = adjoint + forcings[step - 1]
    segment = (column_x * NCT + tile_map).reshape(-1)
    flat_adjoint = jnp.transpose(adjoint, (1, 2, 0, 3)).reshape(NX * NY, 4, NZ)
    sums = jax.ops.segment_sum(flat_adjoint, segment, num_segments=N_GX * NCT).reshape(N_GX, NCT, 4, NZ)
    return (delta + adjoint, alpha + profile_weight * sums)
```

```python
import jax
import jax.numpy as jnp
from jax import lax
from jax.experimental import pallas as pl
from jax.experimental.pallas import tpu as pltpu
from jax.sharding import PartitionSpec as P

STEPS = 3
MESH = pl.DeviceIdType.MESH
f32 = jnp.float32
bf16 = jnp.bfloat16

X0, X1, XB = 4, 20, 24
Y0, Y1, YB = 8, 24, 32

DIRS = [(1, 0), (-1, 0), (0, 1), (0, -1), (1, 1), (1, -1), (-1, 1), (-1, -1)]


def inner_part(sign, lo, hi, width):
    if sign > 0:
        return pl.ds(hi - width, width)
    if sign < 0:
        return pl.ds(lo, width)
    return pl.ds(lo, hi - lo)


def outer_part(sign, lo, hi, width):
    if sign > 0:
        return pl.ds(hi, width)
    if sign < 0:
        return pl.ds(lo - width, width)
    return pl.ds(lo, hi - lo)


def split(value):
    high = value.astype(bf16)
    low = (value - high.astype(f32)).astype(bf16)
    return high, low


def dot(a, b):
    return jnp.dot(a, b, preferred_element_type=f32)


def kernel(
    delta_h, alpha_h, eddy_h, courant_h, tmap_h, obs_h, beam_h, gidx_h, gcol_h, live_h, w_h, prec_h,
    out_d, out_a,
    dl, cf, k5, v0, v1, v2, v3, a1, a2, a3, wv, wc, tm, ov, ob, gbeam, ggate, gcol, glive, gprec,
    al, sums, rsums, rx, ry, rc,
    oh, oht, obh, sel, selt, gmask, scl,
    lsem, asend, arecv, osend, orecv, ysend, yrecv, csend, crecv, hsend, hrecv, psend, precv, ssend, srecv,
):
    nx = lax.axis_size("gx")
    ny = lax.axis_size("gy")
    nz = nx // 2
    ix = lax.axis_index("gx")
    iy = lax.axis_index("gy")
    iz = ix // 2
    il = ix % 2

    local = [
        pltpu.make_async_copy(alpha_h, al.at[iy], lsem.at[0]),
        pltpu.make_async_copy(obs_h, ov, lsem.at[1]),
        pltpu.make_async_copy(eddy_h, cf.at[0, X0:X1, Y0:Y1], lsem.at[2]),
        pltpu.make_async_copy(courant_h, cf.at[pl.ds(1, 2), X0:X1, Y0:Y1], lsem.at[3]),
        pltpu.make_async_copy(tmap_h, tm, lsem.at[4]),
        pltpu.make_async_copy(beam_h, gbeam, lsem.at[5]),
        pltpu.make_async_copy(gidx_h, ggate, lsem.at[6]),
        pltpu.make_async_copy(gcol_h, gcol, lsem.at[7]),
        pltpu.make_async_copy(live_h, glive, lsem.at[8]),
        pltpu.make_async_copy(prec_h, gprec, lsem.at[9]),
        pltpu.make_async_copy(delta_h, dl, lsem.at[10]),
        pltpu.make_async_copy(w_h, wv, lsem.at[11]),
    ]
    for copy in local:
        copy.start()

    def clear_frame(ref, count):
        low = jnp.zeros((count, X0, YB, 128), f32)
        ref[:, 0:X0] = low
        ref[:, X1:XB] = low
        side = jnp.zeros((count, X1 - X0, Y0, 128), f32)
        ref[:, X0:X1, 0:Y0] = side
        ref[:, X0:X1, Y1:YB] = side

    clear_frame(v0, 4)
    clear_frame(cf, 3)
    rx[...] = jnp.zeros_like(rx)
    ry[...] = jnp.zeros_like(ry)
    rc[...] = jnp.zeros_like(rc)

    def there(d):
        dx, dy = DIRS[d]
        ok = None
        for sign, at, count in ((dx, ix, nx), (dy, iy, ny)):
            if sign > 0:
                cond = at < count - 1
            elif sign < 0:
                cond = at > 0
            else:
                continue
            ok = cond if ok is None else jnp.logical_and(ok, cond)
        return ok

    def peer(d):
        dx, dy = DIRS[d]
        return {"gx": ix + dx, "gy": iy + dy}

    barrier = pltpu.get_barrier_semaphore()

    def greet(d, carry):
        pl.semaphore_signal(
            barrier, inc=1, device_id={"gx": ix, "gy": (iy + d) % ny}, device_id_type=MESH
        )
        return carry

    lax.fori_loop(1, ny, greet, 0)

    def greet_z(d, carry):
        pl.semaphore_signal(
            barrier, inc=1, device_id={"gx": ((iz + d) % nz) * 2 + il, "gy": iy}, device_id_type=MESH
        )
        return carry

    lax.fori_loop(1, nz, greet_z, 0)
    expected = (ny - 1) + (nz - 1)
    for d in (0, 1, 4, 5, 6, 7):
        ok = there(d)

        @pl.when(ok)
        def _():
            pl.semaphore_signal(barrier, inc=1, device_id=peer(d), device_id_type=MESH)

        expected = expected + jnp.where(ok, 1, 0)

    local[0].wait()
    local[1].wait()
    for step in range(STEPS):
        ob[il, step, iz] = ov[:, step, :]
    pl.semaphore_wait(barrier, expected)

    def alpha_copy(d):
        return pltpu.make_async_remote_copy(
            src_ref=al.at[iy],
            dst_ref=al.at[iy],
            send_sem=asend.at[d],
            recv_sem=arecv.at[d],
            device_id={"gx": ix, "gy": (iy + d) % ny},
            device_id_type=MESH,
        )

    def alpha_start(d, carry):
        alpha_copy(d).start()
        return carry

    lax.fori_loop(1, ny, alpha_start, 0)

    def obs_copy(d):
        return pltpu.make_async_remote_copy(
            src_ref=ob.at[il, :, iz],
            dst_ref=ob.at[il, :, iz],
            send_sem=osend.at[d],
            recv_sem=orecv.at[d],
            device_id={"gx": ((iz + d) % nz) * 2 + il, "gy": iy},
            device_id_type=MESH,
        )

    def obs_start(d, carry):
        obs_copy(d).start()
        return carry

    lax.fori_loop(1, nz, obs_start, 0)

    def halo_copy(ref, d, width, sends, receives):
        dx, dy = DIRS[d]
        if dx != 0 and dy != 0:
            width = width - 1
        return pltpu.make_async_remote_copy(
            src_ref=ref.at[:, inner_part(dx, X0, X1, width), inner_part(dy, Y0, Y1, width)],
            dst_ref=ref.at[:, outer_part(-dx, X0, X1, width), outer_part(-dy, Y0, Y1, width)],
            send_sem=sends.at[d],
            recv_sem=receives.at[d],
            device_id=peer(d),
            device_id_type=MESH,
        )

    def each(make, act, back):
        for d in range(8):
            dx, dy = DIRS[d]
            here = DIRS.index((-dx, -dy)) if back else d

            @pl.when(there(here))
            def _():
                act(make(d))

    def start(copy):
        copy.start()

    def wait_send(copy):
        copy.wait_send()

    def wait_recv(copy):
        copy.wait_recv()

    def coef_copy(d):
        return halo_copy(cf, d, 2, csend, crecv)

    local[2].wait()
    local[3].wait()
    each(coef_copy, start, False)

    for copy in local[4:10]:
        copy.wait()
    lane = lax.broadcasted_iota(jnp.int32, (256, 128), 1).astype(f32)
    row = lax.broadcasted_iota(jnp.int32, (256, 128), 0)

    def spread(values):
        return jnp.broadcast_to(values, (128, 256)).T

    def hot(values):
        return jnp.concatenate(
            [jnp.where(values == lane, 1.0, 0.0), jnp.where(values == lane + 128.0, 1.0, 0.0)], axis=1
        ).astype(bf16)

    of_row = jnp.where(
        row // 16 == lax.broadcasted_iota(jnp.int32, (256, 128), 1), 1.0, 0.0
    ).astype(bf16)
    of_place = (row % 16) == lax.broadcasted_iota(jnp.int32, (256, 128), 1)
    tiles = jnp.zeros((128, 128), f32)
    tiles = jnp.concatenate(
        [
            jnp.concatenate([tm[...].astype(f32), jnp.zeros((16, 112), f32)], axis=1),
            jnp.zeros((112, 128), f32),
        ],
        axis=0,
    ).astype(bf16)
    picked = jnp.where(of_place, dot(of_row, tiles), 0.0).astype(bf16)
    tile_at = dot(picked, jnp.ones((128, 128), bf16))
    for c in range(4):
        sel[c * 256 : (c + 1) * 256] = hot(tile_at * 4.0 + float(c))

    def alpha_wait(d, carry):
        alpha_copy(d).wait_recv()
        return carry

    local[10].wait()
    lax.fori_loop(1, ny, alpha_wait, 0)
    high, low = split(al[...].reshape(256, 128))
    both = jnp.concatenate([high, low], axis=1)
    for c in range(4):
        product = dot(sel[c * 256 : (c + 1) * 256], both)
        profile = (product[:, :128] + product[:, 128:]).reshape(16, 16, 128)
        v0[c, X0:X1, Y0:Y1] = dl[c] + 0.125 * profile

    def state_copy(d):
        return halo_copy(v0, d, 3, hsend, hrecv)

    each(state_copy, start, False)

    slot_column = gcol[0].astype(f32)
    oh[...] = hot(spread(slot_column))
    up = lax.broadcasted_iota(jnp.int32, (256, 256), 0).astype(f32)
    oht[...] = jnp.where(up == slot_column, 1.0, 0.0).astype(bf16)
    beams = gbeam[0]
    place = ((beams // 8) % 2) * 128 + (beams // 16) * 8 + beams % 8
    obh[...] = hot(spread(place.astype(f32)))
    gmask[...] = jnp.where(spread(ggate[0].astype(f32)) == lane, 1.0, 0.0)
    scl[...] = spread(glive[0].astype(f32) * gprec[0])
    tile_row = tile_at.T[0:1]
    for c in range(4):
        selt[:, c * 256 : (c + 1) * 256] = jnp.where(up == tile_row * 4.0 + float(c), 1.0, 0.0).astype(bf16)
    local[11].wait()
    for c in range(4):
        wc[c] = wv[:, c, :]
    clear_frame(a1, 4)
    clear_frame(a2, 4)
    clear_frame(a3, 4)

    each(coef_copy, wait_recv, True)

    def derive(x, carry):
        e = cf[0, x]
        half_x = 0.5 * cf[1, x]
        half_y = 0.5 * cf[2, x]
        k5[0, x] = 1.0 - 4.0 * e
        k5[1, x] = e - half_x
        k5[2, x] = e + half_x
        k5[3, x] = e - half_y
        k5[4, x] = e + half_y
        return carry

    lax.fori_loop(0, XB, derive, 0)

    def obs_wait(d, carry):
        obs_copy(d).wait_recv()
        return carry

    lax.fori_loop(1, nz, obs_wait, 0)
    relay = pltpu.make_async_remote_copy(
        src_ref=ob.at[il],
        dst_ref=ob.at[il],
        send_sem=ysend,
        recv_sem=yrecv.at[il],
        device_id={"gx": iz * 2 + (1 - il), "gy": iy},
        device_id_type=MESH,
    )
    relay.start()
    incoming = pltpu.make_async_remote_copy(
        src_ref=ob.at[1 - il],
        dst_ref=ob.at[1 - il],
        send_sem=ysend,
        recv_sem=yrecv.at[1 - il],
        device_id={"gx": iz * 2 + (1 - il), "gy": iy},
        device_id_type=MESH,
    )

    each(state_copy, wait_recv, True)

    def forward(src, dst, margin):
        y0, rows = (Y0, 16) if margin == 0 else (4, 24)

        def body(x, carry):
            mid = pl.ds(y0, rows)
            dst[:, x, mid] = (
                k5[0, x, mid] * src[:, x, mid]
                + k5[1, x, mid] * src[:, x + 1, mid]
                + k5[2, x, mid] * src[:, x - 1, mid]
                + k5[3, x, mid] * src[:, x, pl.ds(y0 + 1, rows)]
                + k5[4, x, mid] * src[:, x, pl.ds(y0 - 1, rows)]
            )
            return carry

        lax.fori_loop(X0 - margin, X1 + margin, body, 0)

    def backward(src, dst, margin, extra):
        y0, rows = 4, 24

        def body(x, carry):
            mid = pl.ds(y0, rows)
            below = pl.ds(y0 - 1, rows)
            above = pl.ds(y0 + 1, rows)
            dst[:, x, mid] = (
                k5[0, x, mid] * src[:, x, mid]
                + k5[1, x - 1, mid] * src[:, x - 1, mid]
                + k5[2, x + 1, mid] * src[:, x + 1, mid]
                + k5[3, x, below] * src[:, x, below]
                + k5[4, x, above] * src[:, x, above]
            )
            return carry

        lax.fori_loop(X0 - margin, X1 + margin, body, 0)
        if extra is not None:
            for c in range(4):
                dst[c, X0:X1, Y0:Y1] += extra[c]

    def looked(state):
        parts = [split(state[c, X0:X1, Y0:Y1].reshape(256, 128)) for c in range(4)]
        product = dot(oh[...], jnp.concatenate([h for h, _ in parts] + [l for _, l in parts], axis=1))
        total = None
        for c in range(4):
            term = (product[:, c * 128 : (c + 1) * 128] + product[:, 512 + c * 128 : 640 + c * 128]) * wc[c]
            total = term if total is None else total + term
        return total

    clear_frame(v1, 4)
    clear_frame(v2, 4)
    forward(v0, v1, 2)
    seen = [looked(v1)]
    forward(v1, v2, 1)
    seen.append(looked(v2))
    forward(v2, v3, 0)
    seen.append(looked(v3))

    incoming.wait_recv()
    forcings = []
    for step in range(STEPS):
        high, low = split(ob[:, step].reshape(256, 128))
        product = dot(obh[...], jnp.concatenate([high, low], axis=1))
        observed = (product[:, :128] + product[:, 128:]) * gmask[...]
        misfit = scl[...] * jnp.sum(seen[step] - observed, axis=1, keepdims=True)
        parts = [split(misfit * wc[c]) for c in range(4)]
        product = dot(oht[...], jnp.concatenate([h for h, _ in parts] + [l for _, l in parts], axis=1))
        forcings.append(
            [
                (product[:, c * 128 : (c + 1) * 128] + product[:, 512 + c * 128 : 640 + c * 128]).reshape(16, 16, 128)
                for c in range(4)
            ]
        )
    for c in range(4):
        a3[c, X0:X1, Y0:Y1] = forcings[2][c]
    backward(a3, a2, 1, forcings[1])
    backward(a2, a1, 2, forcings[0])
    backward(a1, v1, 3, None)

    def push_copy(d):
        dx, dy = DIRS[d]
        width = 2 if dx != 0 and dy != 0 else 3
        src = v1.at[:, outer_part(dx, X0, X1, width), outer_part(dy, Y0, Y1, width)]
        at_y = inner_part(-dy, 0, 16, width)
        if dy == 0:
            dst = rx.at[:, inner_part(-dx, 0, 6, width)]
        elif dx == 0:
            dst = ry.at[:, :, at_y]
        else:
            dst = rc.at[:, inner_part(-dx, 0, 4, width), at_y]
        return pltpu.make_async_remote_copy(
            src_ref=src,
            dst_ref=dst,
            send_sem=psend.at[d],
            recv_sem=precv.at[d],
            device_id=peer(d),
            device_id_type=MESH,
        )

    each(push_copy, start, False)
    each(push_copy, wait_recv, True)
    total = None
    for c in range(4):
        v3[c, X0:X1, Y0:Y1] = v1[c, X0:X1, Y0:Y1] + ry[c]
        v3[c, X0 : X0 + 3, Y0:Y1] += rx[c, 0:3]
        v3[c, X1 - 3 : X1, Y0:Y1] += rx[c, 3:6]
        v3[c, X0 : X0 + 2, Y0:Y1] += rc[c, 0:2]
        v3[c, X1 - 2 : X1, Y0:Y1] += rc[c, 2:4]
        high, low = split(v3[c, X0:X1, Y0:Y1].reshape(256, 128))
        product = dot(selt[:, c * 256 : (c + 1) * 256], jnp.concatenate([high, low], axis=1))
        term = product[:, :128] + product[:, 128:]
        total = term if total is None else total + term
    sums[...] = total.reshape(16, 16, 128)

    def sums_copy(d):
        target = (iy + d) % ny
        return pltpu.make_async_remote_copy(
            src_ref=sums.at[target],
            dst_ref=rsums.at[d],
            send_sem=ssend.at[d],
            recv_sem=srecv.at[d],
            device_id={"gx": ix, "gy": target},
            device_id_type=MESH,
        )

    def sums_start(d, carry):
        sums_copy(d).start()
        return carry

    lax.fori_loop(1, ny, sums_start, 0)
    rsums[0] = sums[iy]
    for c in range(4):
        out_d[c] = dl[c] + v3[c, X0:X1, Y0:Y1]

    def finish(d, carry):
        sums_copy(d).wait_recv()
        return carry

    lax.fori_loop(1, ny, finish, 0)
    out_a[...] = al[iy] + 0.125 * jnp.sum(rsums[...], axis=0)

    def sent(d, carry):
        alpha_copy(d).wait_send()
        sums_copy(d).wait_send()
        return carry

    lax.fori_loop(1, ny, sent, 0)

    def sent_z(d, carry):
        obs_copy(d).wait_send()
        return carry

    lax.fori_loop(1, nz, sent_z, 0)
    relay.wait_send()
    each(coef_copy, wait_send, False)
    each(state_copy, wait_send, False)
    each(push_copy, wait_send, False)


def on_device(
    delta, alpha, eddy, courant, tile_map, obs_rows,
    gate_beam, gate_index, gate_column, gate_live, obs_weight, obs_precision,
):
    dma = pltpu.SemaphoreType.DMA
    vm = pltpu.VMEM
    frame = vm((4, XB, YB, 128), f32)
    slots = vm((1, 256), jnp.int32)
    anywhere = pl.BlockSpec(memory_space=pl.ANY)
    inside = pl.BlockSpec(memory_space=pltpu.VMEM)
    row = (1, 256)
    adjoint, grad_alpha = pl.pallas_call(
        kernel,
        out_shape=(
            jax.ShapeDtypeStruct((4, 16, 16, 128), f32),
            jax.ShapeDtypeStruct((16, 128), f32),
        ),
        in_specs=[anywhere] * 12,
        out_specs=(inside, inside),
        scratch_shapes=[
            vm((4, 16, 16, 128), f32),
            vm((3, XB, YB, 128), f32),
            vm((5, XB, YB, 128), f32),
            frame, frame, frame, frame,
            frame, frame, frame,
            vm((256, 4, 128), f32),
            vm((4, 256, 128), f32),
            vm((16, 16), jnp.int32),
            vm((8, 3, 128), f32),
            vm((2, 3, 16, 8, 128), f32),
            slots, slots, slots, slots,
            vm((1, 256), f32),
            vm((16, 16, 128), f32),
            vm((16, 16, 128), f32),
            vm((16, 16, 128), f32),
            vm((4, 6, 16, 128), f32),
            vm((4, 16, 16, 128), f32),
            vm((4, 4, 16, 128), f32),
            vm((256, 256), bf16),
            vm((256, 256), bf16),
            vm((256, 256), bf16),
            vm((1024, 256), bf16),
            vm((256, 1024), bf16),
            vm((256, 128), f32),
            vm((256, 128), f32),
            dma((12,)),
            dma((16,)), dma((16,)),
            dma((16,)), dma((16,)),
            dma, dma((2,)),
            dma((8,)), dma((8,)),
            dma((8,)), dma((8,)),
            dma((8,)), dma((8,)),
            dma((16,)), dma((16,)),
        ],
        compiler_params=pltpu.CompilerParams(
            collective_id=0, has_side_effects=True, vmem_limit_bytes=60 * 1024 * 1024
        ),
    )(
        delta,
        alpha.reshape(16, 128),
        eddy,
        courant,
        tile_map,
        obs_rows,
        gate_beam.reshape(row),
        gate_index.reshape(row),
        gate_column.reshape(row),
        gate_live.reshape(row),
        obs_weight.reshape(256, 4, 128),
        obs_precision.reshape(row),
    )
    return adjoint, grad_alpha.reshape(1, 4, 4, 128)


def solution(mesh):
    return jax.shard_map(
        on_device,
        mesh=mesh,
        in_specs=(
            P(None, "gx", "gy", None),
            P("gx", "gy", None, None),
            P("gx", "gy", None),
            P(None, "gx", "gy", None),
            P("gx", "gy"),
            P(("gx", "gy"), None, None),
            P("gx", "gy", None),
            P("gx", "gy", None),
            P("gx", "gy", None),
            P("gx", "gy", None),
            P("gx", "gy", None, None, None),
            P("gx", "gy", None),
        ),
        out_specs=(P(None, "gx", "gy", None), P("gx", "gy", None, None)),
        check_vma=False,
    )
```

```python
import jax
import jax.numpy as jnp
from jax import lax
from jax.experimental import pallas as pl
from jax.experimental.pallas import tpu as pltpu
from jax.sharding import PartitionSpec as P

STEPS = 3
MESH = pl.DeviceIdType.MESH
f32 = jnp.float32
bf16 = jnp.bfloat16

X0, X1, XB = 4, 20, 24
Y0, Y1, YB = 8, 24, 32

DIRS = [(1, 0), (-1, 0), (0, 1), (0, -1), (1, 1), (1, -1), (-1, 1), (-1, -1)]


def inner_part(sign, lo, hi, width):
    if sign > 0:
        return pl.ds(hi - width, width)
    if sign < 0:
        return pl.ds(lo, width)
    return pl.ds(lo, hi - lo)


def outer_part(sign, lo, hi, width):
    if sign > 0:
        return pl.ds(hi, width)
    if sign < 0:
        return pl.ds(lo - width, width)
    return pl.ds(lo, hi - lo)


def split(value):
    high = value.astype(bf16)
    low = (value - high.astype(f32)).astype(bf16)
    return high, low


def dot(a, b):
    return jnp.dot(a, b, preferred_element_type=f32)


def kernel(
    delta_h, alpha_h, eddy_h, courant_h, tmap_h, obs_h, beam_h, gidx_h, gcol_h, live_h, w_h, prec_h,
    out_d, out_a,
    dl, cf, k5, v0, v1, v2, v3, a1, a2, a3, wv, wc, w2, tm, ob, qi, vo, vi, gcol, glive, gprec,
    al, sums, rsums, rx, ry, rc,
    oh, sel, selt,
    lsem, asend, arecv, osend, orecv, qsend, qrecv, wsend, wrecv,
    csend, crecv, hsend, hrecv, psend, precv, ssend, srecv,
):
    nx = lax.axis_size("gx")
    ny = lax.axis_size("gy")
    nq = nx // 4
    ix = lax.axis_index("gx")
    iy = lax.axis_index("gy")
    iq = ix // 4
    im = ix % 4

    def there(d):
        dx, dy = DIRS[d]
        ok = None
        for sign, at, count in ((dx, ix, nx), (dy, iy, ny)):
            if sign > 0:
                cond = at < count - 1
            elif sign < 0:
                cond = at > 0
            else:
                continue
            ok = cond if ok is None else jnp.logical_and(ok, cond)
        return ok

    def peer(d):
        dx, dy = DIRS[d]
        return {"gx": ix + dx, "gy": iy + dy}

    barrier = pltpu.get_barrier_semaphore()

    def greet(gx, gy):
        pl.semaphore_signal(barrier, inc=1, device_id={"gx": gx, "gy": gy}, device_id_type=MESH)

    for t in range(16):

        @pl.when(t != iy)
        def _():
            greet(ix, t)

    expected = (ny - 1) + 3 + iq
    for d in (0, 1, 4, 5, 6, 7):
        ok = there(d)

        @pl.when(ok)
        def _():
            greet(ix + DIRS[d][0], iy + DIRS[d][1])

        expected = expected + jnp.where(ok, 1, 0)
    for m in range(4):

        @pl.when(m != im)
        def _():
            greet(iq * 4 + m, iy)

    for q in range(1, 8):

        @pl.when(q > iq)
        def _():
            greet(q * 4 + im, iy)

    local = [
        pltpu.make_async_copy(eddy_h, cf.at[0, X0:X1, Y0:Y1], lsem.at[0]),
        pltpu.make_async_copy(courant_h, cf.at[pl.ds(1, 2), X0:X1, Y0:Y1], lsem.at[1]),
        pltpu.make_async_copy(beam_h, qi.at[im, pl.ds(0, 1)], lsem.at[2]),
        pltpu.make_async_copy(gidx_h, qi.at[im, pl.ds(1, 1)], lsem.at[3]),
        pltpu.make_async_copy(tmap_h, tm, lsem.at[4]),
        pltpu.make_async_copy(alpha_h, al.at[iy], lsem.at[5]),
        pltpu.make_async_copy(delta_h, dl, lsem.at[6]),
        pltpu.make_async_copy(gcol_h, gcol, lsem.at[7]),
        pltpu.make_async_copy(live_h, glive, lsem.at[8]),
        pltpu.make_async_copy(prec_h, gprec, lsem.at[9]),
        pltpu.make_async_copy(w_h, wv, lsem.at[10]),
        pltpu.make_async_copy(obs_h, ob.at[iq], lsem.at[11]),
    ]
    for copy in local:
        copy.start()

    def remote(src, dst, send, recv, gx, gy):
        return pltpu.make_async_remote_copy(
            src_ref=src,
            dst_ref=dst,
            send_sem=send,
            recv_sem=recv,
            device_id={"gx": gx, "gy": gy},
            device_id_type=MESH,
        )

    def alpha_out(t):
        return remote(alpha_h, al.at[iy], asend.at[t], arecv.at[iy], ix, t)

    def alpha_in(t):
        return remote(alpha_h, al.at[t], asend.at[t], arecv.at[t], ix, t)

    def obs_out(q):
        return remote(obs_h, ob.at[iq], osend.at[q], orecv.at[iq], q * 4 + im, iy)

    def obs_in(q):
        return remote(obs_h, ob.at[q], osend.at[q], orecv.at[q], q * 4 + im, iy)

    def index_out(m):
        return remote(qi.at[im], qi.at[im], qsend.at[m], qrecv.at[im], iq * 4 + m, iy)

    def index_in(m):
        return remote(qi.at[m], qi.at[m], qsend.at[m], qrecv.at[m], iq * 4 + m, iy)

    def value_out(m):
        return remote(vo.at[m], vi.at[im], wsend.at[m], wrecv.at[im], iq * 4 + m, iy)

    def value_in(m):
        return remote(vo.at[m], vi.at[m], wsend.at[m], wrecv.at[m], iq * 4 + m, iy)

    def sums_out(t):
        return remote(sums.at[t], rsums.at[iy], ssend.at[t], srecv.at[iy], ix, t)

    def sums_in(t):
        return remote(sums.at[t], rsums.at[t], ssend.at[t], srecv.at[t], ix, t)

    def among(count, where, act):
        for t in range(count):

            @pl.when(where(t))
            def _():
                act(t)

    def not_y(t):
        return t != iy

    def not_m(m):
        return m != im

    pl.semaphore_wait(barrier, expected)
    among(16, not_y, lambda t: alpha_out(t).start())
    among(8, lambda q: q < iq, lambda q: obs_out(q).start())

    def halo_copy(ref, d, width, sends, receives):
        dx, dy = DIRS[d]
        if dx != 0 and dy != 0:
            width = width - 1
        gx, gy = ix + dx, iy + dy
        return remote(
            ref.at[:, inner_part(dx, X0, X1, width), inner_part(dy, Y0, Y1, width)],
            ref.at[:, outer_part(-dx, X0, X1, width), outer_part(-dy, Y0, Y1, width)],
            sends.at[d],
            receives.at[d],
            gx,
            gy,
        )

    def each(make, act, back):
        for d in range(8):
            dx, dy = DIRS[d]
            here = DIRS.index((-dx, -dy)) if back else d

            @pl.when(there(here))
            def _():
                act(make(d))

    def start(copy):
        copy.start()

    def wait_send(copy):
        copy.wait_send()

    def wait_recv(copy):
        copy.wait_recv()

    def coef_copy(d):
        return halo_copy(cf, d, 2, csend, crecv)

    def state_copy(d):
        return halo_copy(v0, d, 3, hsend, hrecv)

    local[0].wait()
    local[1].wait()
    each(coef_copy, start, False)
    local[2].wait()
    local[3].wait()
    among(4, not_m, lambda m: index_out(m).start())

    def zero(ref, x, y):
        ref[:, x[0] : x[1], y[0] : y[1]] = jnp.zeros((ref.shape[0], x[1] - x[0], y[1] - y[0], 128), f32)

    def missing(ref, width):
        for d, (dx, dy) in enumerate(DIRS):
            wide = width - 1 if dx != 0 and dy != 0 else width
            spans = []
            for sign, lo, hi in ((dx, X0, X1), (dy, Y0, Y1)):
                spans.append((hi, hi + wide) if sign > 0 else (lo - wide, lo) if sign < 0 else (lo, hi))

            @pl.when(jnp.logical_not(there(d)))
            def _():
                zero(ref, *spans)

    missing(cf, 2)
    missing(v0, 3)
    zero(cf, (0, 2), (0, YB))
    zero(cf, (22, XB), (0, YB))
    zero(cf, (2, 22), (0, 6))
    zero(cf, (2, 22), (26, YB))
    for x in (2, 21):
        zero(cf, (x, x + 1), (6, 8))
        zero(cf, (x, x + 1), (24, 26))
    for x in (3, 20):
        zero(cf, (x, x + 1), (6, 7))
        zero(cf, (x, x + 1), (25, 26))

    local[4].wait()
    lane = lax.broadcasted_iota(jnp.int32, (256, 128), 1)
    row = lax.broadcasted_iota(jnp.int32, (256, 128), 0)
    lanes = lane.astype(f32)
    up = lax.broadcasted_iota(jnp.int32, (256, 256), 0).astype(f32)
    of_row = jnp.where(row // 16 == lane, 1.0, 0.0).astype(bf16)
    tiles = jnp.concatenate(
        [
            jnp.concatenate([tm[...].astype(f32), jnp.zeros((16, 112), f32)], axis=1),
            jnp.zeros((112, 128), f32),
        ],
        axis=0,
    ).astype(bf16)
    picked = jnp.where(row % 16 == lane, dot(of_row, tiles), 0.0).astype(bf16)
    tile_at = dot(picked, jnp.ones((128, 128), bf16)) * 4.0

    def hot(values):
        return jnp.concatenate(
            [jnp.where(values == lanes, 1.0, 0.0), jnp.where(values == lanes + 128.0, 1.0, 0.0)], axis=1
        ).astype(bf16)

    for c in range(4):
        sel[c * 256 : (c + 1) * 256] = hot(tile_at + float(c))
    tile_row = tile_at.T[0:1]
    for c in range(4):
        selt[:, c * 256 : (c + 1) * 256] = jnp.where(up == tile_row + float(c), 1.0, 0.0).astype(bf16)
    for copy in local[5:11]:
        copy.wait()

    among(16, not_y, lambda t: alpha_in(t).wait_recv())
    high, low = split(al[...].reshape(256, 128))
    both = jnp.concatenate([high, low], axis=1)
    for c in range(4):
        product = dot(sel[c * 256 : (c + 1) * 256], both)
        profile = (product[:, :128] + product[:, 128:]).reshape(16, 16, 128)
        v0[c, X0:X1, Y0:Y1] = dl[c] + 0.125 * profile
    each(state_copy, start, False)

    def answer(q):
        obs_in(q).wait_recv()
        obs_out(q).start()

    among(8, lambda q: q > iq, answer)
    slot_column = gcol[0:1].astype(f32)
    oh[...] = jnp.where(up == slot_column, 1.0, 0.0).T.astype(bf16)
    for c in range(4):
        weight = wv[:, c, :]
        high, low = split(weight)
        wc[c] = weight
        w2[:, c * 128 : (c + 1) * 128] = high
        w2[:, 512 + c * 128 : 640 + c * 128] = low
    rx_rows = ((0, 3), (3, 6))
    for d, x in ((0, rx_rows[1]), (1, rx_rows[0])):

        @pl.when(jnp.logical_not(there(d)))
        def _():
            zero(rx, x, (0, 16))

    zero(ry, (0, 16), (3, 13))
    for d, y in ((2, (13, 16)), (3, (0, 3))):

        @pl.when(jnp.logical_not(there(d)))
        def _():
            zero(ry, (0, 16), y)

    zero(rc, (0, 4), (2, 14))
    for d in (4, 5, 6, 7):
        dx, dy = DIRS[d]

        @pl.when(jnp.logical_not(there(d)))
        def _():
            zero(rc, (2, 4) if dx > 0 else (0, 2), (14, 16) if dy > 0 else (0, 2))

    for ref in (a1, a2, a3):
        zero(ref, (0, X0), (0, YB))
        zero(ref, (X1, XB), (0, YB))
        zero(ref, (X0, X1), (0, Y0))
        zero(ref, (X0, X1), (Y1, YB))

    each(coef_copy, wait_recv, True)

    def derive(x, carry):
        e = cf[0, x]
        half_x = 0.5 * cf[1, x]
        half_y = 0.5 * cf[2, x]
        k5[0, x] = 1.0 - 4.0 * e
        k5[1, x] = e - half_x
        k5[2, x] = e + half_x
        k5[3, x] = e - half_y
        k5[4, x] = e + half_y
        return carry

    lax.fori_loop(0, XB, derive, 0)

    among(4, not_m, lambda m: index_in(m).wait_recv())
    local[11].wait()
    among(8, lambda q: q < iq, lambda q: obs_in(q).wait_recv())
    turned = [split(ob[:, step].reshape(64, 128).T) for step in range(STEPS)]
    table = jnp.concatenate([h for h, _ in turned] + [l for _, l in turned], axis=0)
    down64 = lax.broadcasted_iota(jnp.int32, (64, 256), 0)
    down128 = lax.broadcasted_iota(jnp.int32, (128, 256), 0)
    for m in range(4):
        beams = qi[m, 0:1]
        held = jnp.where((beams // 8) % 4 == im, (beams // 32) * 8 + beams % 8, -1)
        found = dot(table, jnp.where(down64 == held, 1.0, 0.0).astype(bf16))
        at_gate = down128 == qi[m, 1:2]
        for step in range(STEPS):
            both = found[step * 128 : (step + 1) * 128] + found[384 + step * 128 : 512 + step * 128]
            vo[m, step : step + 1] = jnp.sum(jnp.where(at_gate, both, 0.0), axis=0, keepdims=True)
    among(4, not_m, lambda m: value_out(m).start())

    each(state_copy, wait_recv, True)

    def forward(src, dst, margin):
        y0, rows = (Y0, 16) if margin == 0 else (4, 24)

        def body(x, carry):
            mid = pl.ds(y0, rows)
            dst[:, x, mid] = (
                k5[0, x, mid] * src[:, x, mid]
                + k5[1, x, mid] * src[:, x + 1, mid]
                + k5[2, x, mid] * src[:, x - 1, mid]
                + k5[3, x, mid] * src[:, x, pl.ds(y0 + 1, rows)]
                + k5[4, x, mid] * src[:, x, pl.ds(y0 - 1, rows)]
            )
            return carry

        lax.fori_loop(X0 - margin, X1 + margin, body, 0)

    def backward(src, dst, margin, extra):
        y0, rows = 4, 24

        def body(x, carry):
            mid = pl.ds(y0, rows)
            below = pl.ds(y0 - 1, rows)
            above = pl.ds(y0 + 1, rows)
            dst[:, x, mid] = (
                k5[0, x, mid] * src[:, x, mid]
                + k5[1, x - 1, mid] * src[:, x - 1, mid]
                + k5[2, x + 1, mid] * src[:, x + 1, mid]
                + k5[3, x, below] * src[:, x, below]
                + k5[4, x, above] * src[:, x, above]
            )
            return carry

        lax.fori_loop(X0 - margin, X1 + margin, body, 0)
        if extra is not None:
            for c in range(4):
                dst[c, X0:X1, Y0:Y1] += extra[c]

    ones = jnp.ones((8, 128), bf16)

    def along(value):
        return lax.dot_general(ones, value, (((1,), (1,)), ((), ())), preferred_element_type=f32)[0:1]

    def looked(state):
        parts = [split(state[c, X0:X1, Y0:Y1].reshape(256, 128)) for c in range(4)]
        product = dot(oh[...], jnp.concatenate([h for h, _ in parts] + [l for _, l in parts], axis=1))
        total = None
        for c in range(4):
            term = (product[:, c * 128 : (c + 1) * 128] + product[:, 512 + c * 128 : 640 + c * 128]) * wc[c]
            total = term if total is None else total + term
        high, low = split(total)
        return along(high) + along(low)

    forward(v0, v1, 2)
    seen = [looked(v1)]
    forward(v1, v2, 1)
    seen.append(looked(v2))
    forward(v2, v3, 0)
    seen.append(looked(v3))

    among(4, not_m, lambda m: value_in(m).wait_recv())
    vi[im] = vo[im]
    scale = glive[...].astype(f32) * gprec[...]
    mask = up == slot_column

    def forcing(step):
        observed = vi[0, step : step + 1] + vi[1, step : step + 1] + vi[2, step : step + 1] + vi[3, step : step + 1]
        misfit = scale * (seen[step] - observed)
        coarse = misfit.astype(bf16).astype(f32)
        fine = misfit - coarse
        wide = dot(jnp.where(mask, coarse, 0.0).astype(bf16), w2[...])
        rest = dot(jnp.where(mask, fine, 0.0).astype(bf16), w2[:, :512])
        return [
            (
                wide[:, c * 128 : (c + 1) * 128]
                + wide[:, 512 + c * 128 : 640 + c * 128]
                + rest[:, c * 128 : (c + 1) * 128]
            ).reshape(16, 16, 128)
            for c in range(4)
        ]

    last = forcing(2)
    for c in range(4):
        a3[c, X0:X1, Y0:Y1] = last[c]
    backward(a3, a2, 1, forcing(1))
    backward(a2, a1, 2, forcing(0))
    backward(a1, v1, 3, None)

    def push_copy(d):
        dx, dy = DIRS[d]
        width = 2 if dx != 0 and dy != 0 else 3
        src = v1.at[:, outer_part(dx, X0, X1, width), outer_part(dy, Y0, Y1, width)]
        at_y = inner_part(-dy, 0, 16, width)
        if dy == 0:
            dst = rx.at[:, inner_part(-dx, 0, 6, width)]
        elif dx == 0:
            dst = ry.at[:, :, at_y]
        else:
            dst = rc.at[:, inner_part(-dx, 0, 4, width), at_y]
        return remote(src, dst, psend.at[d], precv.at[d], ix + dx, iy + dy)

    each(push_copy, start, False)
    each(push_copy, wait_recv, True)
    total = None
    for c in range(4):
        v3[c, X0:X1, Y0:Y1] = v1[c, X0:X1, Y0:Y1] + ry[c]
        v3[c, X0 : X0 + 3, Y0:Y1] += rx[c, 0:3]
        v3[c, X1 - 3 : X1, Y0:Y1] += rx[c, 3:6]
        v3[c, X0 : X0 + 2, Y0:Y1] += rc[c, 0:2]
        v3[c, X1 - 2 : X1, Y0:Y1] += rc[c, 2:4]
        high, low = split(v3[c, X0:X1, Y0:Y1].reshape(256, 128))
        product = dot(selt[:, c * 256 : (c + 1) * 256], jnp.concatenate([high, low], axis=1))
        term = product[:, :128] + product[:, 128:]
        total = term if total is None else total + term
    sums[...] = total.reshape(16, 16, 128)
    among(16, not_y, lambda t: sums_out(t).start())
    rsums[iy] = sums[iy]
    for c in range(4):
        out_d[c] = dl[c] + v3[c, X0:X1, Y0:Y1]
    among(16, not_y, lambda t: alpha_out(t).wait_send())
    among(8, lambda q: q != iq, lambda q: obs_out(q).wait_send())
    among(4, not_m, lambda m: index_out(m).wait_send())
    among(4, not_m, lambda m: value_out(m).wait_send())
    each(coef_copy, wait_send, False)
    each(state_copy, wait_send, False)
    each(push_copy, wait_send, False)
    among(16, not_y, lambda t: sums_in(t).wait_recv())
    result = al[iy] + 0.125 * jnp.sum(rsums[...], axis=0)
    for t in range(4):
        out_a[t] = result[4 * t : 4 * t + 4]
    among(16, not_y, lambda t: sums_out(t).wait_send())


def on_device(
    delta, alpha, eddy, courant, tile_map, obs_rows,
    gate_beam, gate_index, gate_column, gate_live, obs_weight, obs_precision,
):
    dma = pltpu.SemaphoreType.DMA
    vm = pltpu.VMEM
    frame = vm((4, XB, YB, 128), f32)
    slots = vm((1, 256), jnp.int32)
    anywhere = pl.BlockSpec(memory_space=pl.ANY)
    inside = pl.BlockSpec(memory_space=pltpu.VMEM)
    row = (1, 256)
    adjoint, grad_alpha = pl.pallas_call(
        kernel,
        out_shape=(
            jax.ShapeDtypeStruct((4, 16, 16, 128), f32),
            jax.ShapeDtypeStruct((4, 4, 128), f32),
        ),
        in_specs=[anywhere] * 12,
        out_specs=(inside, inside),
        scratch_shapes=[
            vm((4, 16, 16, 128), f32),
            vm((3, XB, YB, 128), f32),
            vm((5, XB, YB, 128), f32),
            frame, frame, frame, frame,
            frame, frame, frame,
            vm((256, 4, 128), f32),
            vm((4, 256, 128), f32),
            vm((256, 1024), bf16),
            vm((16, 16), jnp.int32),
            vm((8, 3, 8, 128), f32),
            vm((4, 2, 256), jnp.int32),
            vm((4, 3, 256), f32),
            vm((4, 3, 256), f32),
            slots, slots,
            vm((1, 256), f32),
            vm((16, 16, 128), f32),
            vm((16, 16, 128), f32),
            vm((16, 16, 128), f32),
            vm((4, 6, 16, 128), f32),
            vm((4, 16, 16, 128), f32),
            vm((4, 4, 16, 128), f32),
            vm((256, 256), bf16),
            vm((1024, 256), bf16),
            vm((256, 1024), bf16),
            dma((12,)),
            dma((16,)), dma((16,)),
            dma((8,)), dma((8,)),
            dma((4,)), dma((4,)),
            dma((4,)), dma((4,)),
            dma((8,)), dma((8,)),
            dma((8,)), dma((8,)),
            dma((8,)), dma((8,)),
            dma((16,)), dma((16,)),
        ],
        compiler_params=pltpu.CompilerParams(
            collective_id=0, has_side_effects=True, vmem_limit_bytes=60 * 1024 * 1024
        ),
    )(
        delta,
        alpha.reshape(16, 128),
        eddy,
        courant,
        tile_map,
        obs_rows.transpose(1, 0, 2),
        gate_beam.reshape(row),
        gate_index.reshape(row),
        gate_column.reshape(row),
        gate_live.reshape(row),
        obs_weight.reshape(256, 4, 128),
        obs_precision.reshape(row),
    )
    return adjoint, grad_alpha.reshape(1, 4, 4, 128)


def solution(mesh):
    return jax.shard_map(
        on_device,
        mesh=mesh,
        in_specs=(
            P(None, "gx", "gy", None),
            P("gx", "gy", None, None),
            P("gx", "gy", None),
            P(None, "gx", "gy", None),
            P("gx", "gy"),
            P(("gx", "gy"), None, None),
            P("gx", "gy", None),
            P("gx", "gy", None),
            P("gx", "gy", None),
            P("gx", "gy", None),
            P("gx", "gy", None, None, None),
            P("gx", "gy", None),
        ),
        out_specs=(P(None, "gx", "gy", None), P("gx", "gy", None, None)),
        check_vma=False,
    )
```

```python
import jax
import jax.numpy as jnp
from jax import lax
from jax.experimental import pallas as pl
from jax.experimental.pallas import tpu as pltpu
from jax.sharding import PartitionSpec as P

STEPS = 3
MESH = pl.DeviceIdType.MESH
f32 = jnp.float32
bf16 = jnp.bfloat16

X0, X1, XB = 4, 20, 24
Y0, Y1, YB = 8, 24, 32

DIRS = [(1, 0), (-1, 0), (0, 1), (0, -1), (1, 1), (1, -1), (-1, 1), (-1, -1)]


EDGES = (0, 1, 4, 5, 6, 7)
SIDES = (2, 3)


def inner_part(sign, lo, hi, width):
    if sign > 0:
        return pl.ds(hi - width, width)
    if sign < 0:
        return pl.ds(lo, width)
    return pl.ds(lo, hi - lo)


def outer_part(sign, lo, hi, width):
    if sign > 0:
        return pl.ds(hi, width)
    if sign < 0:
        return pl.ds(lo - width, width)
    return pl.ds(lo, hi - lo)


def split(value):
    high = value.astype(bf16)
    low = (value - high.astype(f32)).astype(bf16)
    return high, low


def dot(a, b):
    return jnp.dot(a, b, preferred_element_type=f32)


AT_ONCE = ((), (0,), (0, 1), (0, 1, 2), (0, 1, 2, 3, 5, 6), (0, 1, 2, 3, 4, 6, 7), (0, 1, 4, 5, 7), (0, 1, 2, 5, 6))
THROUGH = ((), (), (), (), ((5, 7),), (), ((5, 3), (4, 2)), ((6, 4), (5, 3)))
ANSWER = tuple(tuple(range(q + 1, 8)) if q < 4 else () for q in range(8))


def kernel(
    delta_h, alpha_h, eddy_h, courant_h, tmap_h, obs_h, beam_h, gidx_h, gcol_h, live_h, w_h, prec_h,
    out_d, out_a,
    od, oa, dl, cf, k5, v0, v1, v2, v3, a1, a2, a3, wv, wc, w2, tm, ob, qi, vo, vi, gcol, glive, gprec,
    al, sums, rsums, rx, ry, rc,
    oh, sel, selt,
    lsem, asend, arecv, osend, orecv, qsend, qrecv, wsend, wrecv,
    csend, crecv, hsend, hrecv, psend, precv, ssend, srecv,
):
    nx = lax.axis_size("gx")
    ny = lax.axis_size("gy")
    nq = nx // 4
    ix = lax.axis_index("gx")
    iy = lax.axis_index("gy")
    iq = ix // 4
    im = ix % 4

    def there(d):
        dx, dy = DIRS[d]
        ok = None
        for sign, at, count in ((dx, ix, nx), (dy, iy, ny)):
            if sign > 0:
                cond = at < count - 1
            elif sign < 0:
                cond = at > 0
            else:
                continue
            ok = cond if ok is None else jnp.logical_and(ok, cond)
        return ok

    def peer(d):
        dx, dy = DIRS[d]
        return {"gx": ix + dx, "gy": iy + dy}

    barrier = pltpu.get_barrier_semaphore()

    def greet(gx, gy):
        pl.semaphore_signal(barrier, inc=1, device_id={"gx": gx, "gy": gy}, device_id_type=MESH)

    for t in range(16):

        @pl.when(t != iy)
        def _():
            greet(ix, t)

    greeted = 0
    for q in range(8):
        greeted = greeted + jnp.where(iq == q, len(AT_ONCE[q]), 0)
    expected = (ny - 1) + 3 + greeted
    for d in (0, 1, 4, 5, 6, 7):
        ok = there(d)

        @pl.when(ok)
        def _():
            greet(ix + DIRS[d][0], iy + DIRS[d][1])

        expected = expected + jnp.where(ok, 1, 0)
    for m in range(4):

        @pl.when(m != im)
        def _():
            greet(iq * 4 + m, iy)

    def far(table, act):
        for q in range(8):
            if table[q]:

                @pl.when(iq == q)
                def _():
                    for item in table[q]:
                        act(item)

    far([[r for r in range(8) if q in AT_ONCE[r]] for q in range(8)], lambda r: greet(r * 4 + im, iy))

    local = [
        pltpu.make_async_copy(alpha_h, al.at[iy], lsem.at[0]),
        pltpu.make_async_copy(obs_h, ob.at[iq], lsem.at[1]),
        pltpu.make_async_copy(eddy_h, cf.at[0, X0:X1, Y0:Y1], lsem.at[2]),
        pltpu.make_async_copy(courant_h, cf.at[pl.ds(1, 2), X0:X1, Y0:Y1], lsem.at[3]),
        pltpu.make_async_copy(beam_h, qi.at[im, pl.ds(0, 1)], lsem.at[4]),
        pltpu.make_async_copy(gidx_h, qi.at[im, pl.ds(1, 1)], lsem.at[5]),
        pltpu.make_async_copy(tmap_h, tm, lsem.at[6]),
        pltpu.make_async_copy(gcol_h, gcol, lsem.at[7]),
        pltpu.make_async_copy(live_h, glive, lsem.at[8]),
        pltpu.make_async_copy(prec_h, gprec, lsem.at[9]),
        pltpu.make_async_copy(w_h, wv, lsem.at[10]),
        pltpu.make_async_copy(delta_h, dl, lsem.at[11]),
    ]
    for copy in local:
        copy.start()

    def remote(src, dst, send, recv, gx, gy):
        return pltpu.make_async_remote_copy(
            src_ref=src,
            dst_ref=dst,
            send_sem=send,
            recv_sem=recv,
            device_id={"gx": gx, "gy": gy},
            device_id_type=MESH,
        )

    def alpha_out(t):
        return remote(al.at[iy], al.at[iy], asend.at[t], arecv.at[iy], ix, t)

    def alpha_in(t):
        return remote(al.at[t], al.at[t], asend.at[t], arecv.at[t], ix, t)

    def obs_out(q):
        return remote(ob.at[iq], ob.at[iq], osend.at[q], orecv.at[iq], q * 4 + im, iy)

    def obs_in(q):
        return remote(ob.at[q], ob.at[q], osend.at[q], orecv.at[q], q * 4 + im, iy)

    def index_out(m):
        return remote(qi.at[im], qi.at[im], qsend.at[m], qrecv.at[im], iq * 4 + m, iy)

    def index_in(m):
        return remote(qi.at[m], qi.at[m], qsend.at[m], qrecv.at[m], iq * 4 + m, iy)

    def value_out(m):
        return remote(vo.at[m], vi.at[im], wsend.at[m], wrecv.at[im], iq * 4 + m, iy)

    def value_in(m):
        return remote(vo.at[m], vi.at[m], wsend.at[m], wrecv.at[m], iq * 4 + m, iy)

    def sums_out(t):
        return remote(sums.at[t], rsums.at[iy], ssend.at[t], srecv.at[iy], ix, t)

    def sums_in(t):
        return remote(sums.at[t], rsums.at[t], ssend.at[t], srecv.at[t], ix, t)

    def among(count, where, act):
        for t in range(count):

            @pl.when(where(t))
            def _():
                act(t)

    ox = (iy // 2) % 4
    others = []
    for dy, dx in ((1, 2), (1, 1), (1, 3), (0, 2), (1, 0), (0, 1), (0, 3), (0, 0)):
        for dc in (1, 0):
            if (dy, dx, dc) != (0, 0, 0):
                ty = (iy // 8 + dy) % 2
                others.append(ty * 8 + ((ox + dx) % 4) * 2 + (iy + dc) % 2)

    def strip(act):
        for t in others:
            act(t)

    def not_m(m):
        return m != im

    local[0].wait()
    local[1].wait()
    pl.semaphore_wait(barrier, expected)
    strip(lambda t: alpha_out(t).start())
    far(AT_ONCE, lambda q: obs_out(q).start())

    def halo_copy(ref, d, width, sends, receives):
        dx, dy = DIRS[d]
        if dx != 0 and dy != 0:
            width = width - 1
        gx, gy = ix + dx, iy + dy
        return remote(
            ref.at[:, inner_part(dx, X0, X1, width), inner_part(dy, Y0, Y1, width)],
            ref.at[:, outer_part(-dx, X0, X1, width), outer_part(-dy, Y0, Y1, width)],
            sends.at[d],
            receives.at[d],
            gx,
            gy,
        )

    def each(make, act, back, those=range(8)):
        for d in those:
            dx, dy = DIRS[d]
            here = DIRS.index((-dx, -dy)) if back else d

            @pl.when(there(here))
            def _():
                act(make(d))

    def start(copy):
        copy.start()

    def wait_send(copy):
        copy.wait_send()

    def wait_recv(copy):
        copy.wait_recv()

    def coef_copy(d):
        return halo_copy(cf, d, 2, csend, crecv)

    def state_copy(d):
        return halo_copy(v0, d, 3, hsend, hrecv)

    local[2].wait()
    local[3].wait()
    each(coef_copy, start, False)
    local[4].wait()
    local[5].wait()
    among(4, not_m, lambda m: index_out(m).start())

    def zero(ref, x, y):
        ref[:, x[0] : x[1], y[0] : y[1]] = jnp.zeros((ref.shape[0], x[1] - x[0], y[1] - y[0], 128), f32)

    def missing(ref, width):
        for d, (dx, dy) in enumerate(DIRS):
            wide = width - 1 if dx != 0 and dy != 0 else width
            spans = []
            for sign, lo, hi in ((dx, X0, X1), (dy, Y0, Y1)):
                spans.append((hi, hi + wide) if sign > 0 else (lo - wide, lo) if sign < 0 else (lo, hi))

            @pl.when(jnp.logical_not(there(d)))
            def _():
                zero(ref, *spans)

    missing(cf, 2)
    missing(v0, 3)
    zero(cf, (0, 2), (0, YB))
    zero(cf, (22, XB), (0, YB))
    zero(cf, (2, 22), (0, 6))
    zero(cf, (2, 22), (26, YB))
    for x in (2, 21):
        zero(cf, (x, x + 1), (6, 8))
        zero(cf, (x, x + 1), (24, 26))
    for x in (3, 20):
        zero(cf, (x, x + 1), (6, 7))
        zero(cf, (x, x + 1), (25, 26))

    local[6].wait()
    lane = lax.broadcasted_iota(jnp.int32, (256, 128), 1)
    row = lax.broadcasted_iota(jnp.int32, (256, 128), 0)
    lanes = lane.astype(f32)
    up = lax.broadcasted_iota(jnp.int32, (256, 256), 0).astype(f32)
    of_row = jnp.where(row // 16 == lane, 1.0, 0.0).astype(bf16)
    tiles = jnp.concatenate(
        [
            jnp.concatenate([tm[...].astype(f32), jnp.zeros((16, 112), f32)], axis=1),
            jnp.zeros((112, 128), f32),
        ],
        axis=0,
    ).astype(bf16)
    picked = jnp.where(row % 16 == lane, dot(of_row, tiles), 0.0).astype(bf16)
    tile_at = dot(picked, jnp.ones((128, 128), bf16)) * 4.0

    def hot(values):
        return jnp.concatenate(
            [jnp.where(values == lanes, 1.0, 0.0), jnp.where(values == lanes + 128.0, 1.0, 0.0)], axis=1
        ).astype(bf16)

    for c in range(4):
        sel[c * 256 : (c + 1) * 256] = hot(tile_at + float(c))
    tile_row = tile_at.T[0:1]
    for c in range(4):
        selt[:, c * 256 : (c + 1) * 256] = jnp.where(up == tile_row + float(c), 1.0, 0.0).astype(bf16)
    for copy in local[7:12]:
        copy.wait()

    slot_column = gcol[0:1].astype(f32)
    at_slot = jnp.where(up == slot_column, 1.0, 0.0).T.astype(bf16)
    oh[:, :256] = at_slot
    oh[:, 256:] = at_slot
    for c in range(4):
        weight = wv[:, c, :]
        high, low = split(weight)
        wc[c] = weight
        w2[0:256, c * 128 : (c + 1) * 128] = high
        w2[256:512, c * 128 : (c + 1) * 128] = low
        w2[512:768, c * 128 : (c + 1) * 128] = high
    rx_rows = ((0, 3), (3, 6))
    for d, x in ((0, rx_rows[1]), (1, rx_rows[0])):

        @pl.when(jnp.logical_not(there(d)))
        def _():
            zero(rx, x, (0, 16))

    zero(ry, (0, 16), (3, 13))
    for d, y in ((2, (13, 16)), (3, (0, 3))):

        @pl.when(jnp.logical_not(there(d)))
        def _():
            zero(ry, (0, 16), y)

    zero(rc, (0, 4), (2, 14))
    for d in (4, 5, 6, 7):
        dx, dy = DIRS[d]

        @pl.when(jnp.logical_not(there(d)))
        def _():
            zero(rc, (2, 4) if dx > 0 else (0, 2), (14, 16) if dy > 0 else (0, 2))

    for ref in (a1, a2, a3):
        zero(ref, (0, X0), (0, YB))
        zero(ref, (X1, XB), (0, YB))
        zero(ref, (X0, X1), (0, Y0))
        zero(ref, (X0, X1), (Y1, YB))

    def through(item):
        obs_in(item[0]).wait_recv()
        obs_out(item[1]).start()

    far(THROUGH, through)

    strip(lambda t: alpha_in(t).wait_recv())
    high, low = split(al[...].reshape(256, 128))
    both = jnp.concatenate([high, low], axis=1)

    def state_rows(x0, x1):
        for c in range(4):
            product = dot(sel[c * 256 + x0 * 16 : c * 256 + x1 * 16], both)
            profile = (product[:, :128] + product[:, 128:]).reshape(x1 - x0, 16, 128)
            v0[c, X0 + x0 : X0 + x1, Y0:Y1] = dl[c, x0:x1] + 0.125 * profile

    state_rows(0, 3)
    state_rows(13, 16)
    each(state_copy, start, False, EDGES)
    state_rows(3, 13)
    each(state_copy, start, False, SIDES)

    each(coef_copy, wait_recv, True)

    def derive(x, carry):
        e = cf[0, x]
        half_x = 0.5 * cf[1, x]
        half_y = 0.5 * cf[2, x]
        k5[0, x] = 1.0 - 4.0 * e
        k5[1, x] = e - half_x
        k5[2, x] = e + half_x
        k5[3, x] = e - half_y
        k5[4, x] = e + half_y
        return carry

    lax.fori_loop(0, XB, derive, 0)

    def answer(q):
        obs_in(q).wait_recv()
        obs_out(q).start()

    far(ANSWER, answer)
    among(4, not_m, lambda m: index_in(m).wait_recv())
    waited = [[t for t, _ in THROUGH[q]] + list(ANSWER[q]) + [q] for q in range(8)]
    far([[r for r in range(8) if r not in waited[q]] for q in range(8)], lambda q: obs_in(q).wait_recv())
    turned = [split(ob[:, step].reshape(64, 128).T) for step in range(STEPS)]
    table = jnp.concatenate([jnp.concatenate(pair, axis=1) for pair in turned], axis=0)
    down64 = lax.broadcasted_iota(jnp.int32, (64, 256), 0)
    down128 = lax.broadcasted_iota(jnp.int32, (128, 256), 0)
    for m in range(4):
        beams = qi[m, 0:1]
        held = jnp.where((beams // 8) % 4 == im, (beams // 32) * 8 + beams % 8, -1)
        at_beam = jnp.where(down64 == held, 1.0, 0.0).astype(bf16)
        found = dot(table, jnp.concatenate([at_beam, at_beam], axis=0))
        at_gate = down128 == qi[m, 1:2]
        for step in range(STEPS):
            both = found[step * 128 : (step + 1) * 128]
            vo[m, step : step + 1] = jnp.sum(jnp.where(at_gate, both, 0.0), axis=0, keepdims=True)
    among(4, not_m, lambda m: value_out(m).start())

    each(state_copy, wait_recv, True)

    def forward(src, dst, margin):
        y0, rows = (Y0, 16) if margin == 0 else (4, 24)

        def body(x, carry):
            mid = pl.ds(y0, rows)
            dst[:, x, mid] = (
                k5[0, x, mid] * src[:, x, mid]
                + k5[1, x, mid] * src[:, x + 1, mid]
                + k5[2, x, mid] * src[:, x - 1, mid]
                + k5[3, x, mid] * src[:, x, pl.ds(y0 + 1, rows)]
                + k5[4, x, mid] * src[:, x, pl.ds(y0 - 1, rows)]
            )
            return carry

        lax.fori_loop(X0 - margin, X1 + margin, body, 0)

    def backward(src, dst, first, last, extra):
        y0, rows = 4, 24

        def body(x, carry):
            mid = pl.ds(y0, rows)
            below = pl.ds(y0 - 1, rows)
            above = pl.ds(y0 + 1, rows)
            dst[:, x, mid] = (
                k5[0, x, mid] * src[:, x, mid]
                + k5[1, x - 1, mid] * src[:, x - 1, mid]
                + k5[2, x + 1, mid] * src[:, x + 1, mid]
                + k5[3, x, below] * src[:, x, below]
                + k5[4, x, above] * src[:, x, above]
            )
            return carry

        lax.fori_loop(first, last, body, 0)
        if extra is not None:
            for c in range(4):
                dst[c, X0:X1, Y0:Y1] += extra[c]

    ones = jnp.ones((8, 128), bf16)

    def along(value):
        return lax.dot_general(ones, value, (((1,), (1,)), ((), ())), preferred_element_type=f32)[0:1]

    def looked(state):
        parts = [split(state[c, X0:X1, Y0:Y1].reshape(256, 128)) for c in range(4)]
        halves = [jnp.concatenate([part[k] for part in parts], axis=1) for k in range(2)]
        product = dot(oh[...], jnp.concatenate(halves, axis=0))
        total = None
        for c in range(4):
            term = product[:, c * 128 : (c + 1) * 128] * wc[c]
            total = term if total is None else total + term
        high, low = split(total)
        return along(high) + along(low)

    forward(v0, v1, 2)
    seen = [looked(v1)]
    forward(v1, v2, 1)
    seen.append(looked(v2))
    forward(v2, v3, 0)
    seen.append(looked(v3))

    among(4, not_m, lambda m: value_in(m).wait_recv())
    vi[im] = vo[im]
    scale = glive[...].astype(f32) * gprec[...]
    mask = up == slot_column

    def forcing(step):
        observed = vi[0, step : step + 1] + vi[1, step : step + 1] + vi[2, step : step + 1] + vi[3, step : step + 1]
        misfit = scale * (seen[step] - observed)
        coarse = misfit.astype(bf16).astype(f32)
        fine = misfit - coarse
        high = jnp.where(mask, coarse, 0.0).astype(bf16)
        low = jnp.where(mask, fine, 0.0).astype(bf16)
        product = dot(jnp.concatenate([high, high, low], axis=1), w2[...])
        return [product[:, c * 128 : (c + 1) * 128].reshape(16, 16, 128) for c in range(4)]

    last = forcing(2)
    for c in range(4):
        a3[c, X0:X1, Y0:Y1] = last[c]
    backward(a3, a2, X0 - 1, X1 + 1, forcing(1))
    backward(a2, a1, X0 - 2, X1 + 2, forcing(0))
    backward(a1, v1, X0 - 3, X0, None)
    backward(a1, v1, X1, X1 + 3, None)

    def push_copy(d):
        dx, dy = DIRS[d]
        width = 2 if dx != 0 and dy != 0 else 3
        src = v1.at[:, outer_part(dx, X0, X1, width), outer_part(dy, Y0, Y1, width)]
        at_y = inner_part(-dy, 0, 16, width)
        if dy == 0:
            dst = rx.at[:, inner_part(-dx, 0, 6, width)]
        elif dx == 0:
            dst = ry.at[:, :, at_y]
        else:
            dst = rc.at[:, inner_part(-dx, 0, 4, width), at_y]
        return remote(src, dst, psend.at[d], precv.at[d], ix + dx, iy + dy)

    each(push_copy, start, False, EDGES)
    backward(a1, v1, X0, X1, None)
    each(push_copy, start, False, SIDES)
    each(push_copy, wait_recv, True)
    total = None
    for c in range(4):
        v3[c, X0:X1, Y0:Y1] = v1[c, X0:X1, Y0:Y1] + ry[c]
        v3[c, X0 : X0 + 3, Y0:Y1] += rx[c, 0:3]
        v3[c, X1 - 3 : X1, Y0:Y1] += rx[c, 3:6]
        v3[c, X0 : X0 + 2, Y0:Y1] += rc[c, 0:2]
        v3[c, X1 - 2 : X1, Y0:Y1] += rc[c, 2:4]
        high, low = split(v3[c, X0:X1, Y0:Y1].reshape(256, 128))
        product = dot(selt[:, c * 256 : (c + 1) * 256], jnp.concatenate([high, low], axis=1))
        term = product[:, :128] + product[:, 128:]
        total = term if total is None else total + term
    sums[...] = total.reshape(16, 16, 128)
    strip(lambda t: sums_out(t).start())
    rsums[iy] = sums[iy]
    for c in range(4):
        od[c] = dl[c] + v3[c, X0:X1, Y0:Y1]
    leave_d = pltpu.make_async_copy(od, out_d, lsem.at[0])
    leave_d.start()
    strip(lambda t: alpha_out(t).wait_send())
    among(8, lambda q: q != iq, lambda q: obs_out(q).wait_send())
    among(4, not_m, lambda m: index_out(m).wait_send())
    among(4, not_m, lambda m: value_out(m).wait_send())
    each(coef_copy, wait_send, False)
    each(state_copy, wait_send, False)
    each(push_copy, wait_send, False)
    strip(lambda t: sums_in(t).wait_recv())
    result = al[iy] + 0.125 * jnp.sum(rsums[...], axis=0)
    for t in range(4):
        oa[t] = result[4 * t : 4 * t + 4]
    leave_a = pltpu.make_async_copy(oa, out_a, lsem.at[1])
    leave_a.start()
    strip(lambda t: sums_out(t).wait_send())
    leave_d.wait()
    leave_a.wait()


def hand_on(d_ref, a_ref, out_d, out_a, sems):
    copies = [pltpu.make_async_copy(d_ref, out_d, sems.at[0]), pltpu.make_async_copy(a_ref, out_a, sems.at[1])]
    for copy in copies:
        copy.start()
    for copy in copies:
        copy.wait()


def on_device(
    delta, alpha, eddy, courant, tile_map, obs_rows,
    gate_beam, gate_index, gate_column, gate_live, obs_weight, obs_precision,
):
    dma = pltpu.SemaphoreType.DMA
    vm = pltpu.VMEM
    frame = vm((4, XB, YB, 128), f32)
    slots = vm((1, 256), jnp.int32)
    anywhere = pl.BlockSpec(memory_space=pl.ANY)
    row = (1, 256)
    grad_delta, grad_alpha = pl.pallas_call(
        kernel,
        out_shape=(
            jax.ShapeDtypeStruct((4, 16, 16, 128), f32),
            jax.ShapeDtypeStruct((4, 4, 128), f32),
        ),
        in_specs=[anywhere] * 12,
        out_specs=(anywhere, anywhere),
        scratch_shapes=[
            vm((4, 16, 16, 128), f32),
            vm((4, 4, 128), f32),
            vm((4, 16, 16, 128), f32),
            vm((3, XB, YB, 128), f32),
            vm((5, XB, YB, 128), f32),
            frame, frame, frame, frame,
            frame, frame, frame,
            vm((256, 4, 128), f32),
            vm((4, 256, 128), f32),
            vm((768, 512), bf16),
            vm((16, 16), jnp.int32),
            vm((8, 3, 8, 128), f32),
            vm((4, 2, 256), jnp.int32),
            vm((4, 3, 256), f32),
            vm((4, 3, 256), f32),
            slots, slots,
            vm((1, 256), f32),
            vm((16, 16, 128), f32),
            vm((16, 16, 128), f32),
            vm((16, 16, 128), f32),
            vm((4, 6, 16, 128), f32),
            vm((4, 16, 16, 128), f32),
            vm((4, 4, 16, 128), f32),
            vm((256, 512), bf16),
            vm((1024, 256), bf16),
            vm((256, 1024), bf16),
            dma((12,)),
            dma((16,)), dma((16,)),
            dma((8,)), dma((8,)),
            dma((4,)), dma((4,)),
            dma((4,)), dma((4,)),
            dma((8,)), dma((8,)),
            dma((8,)), dma((8,)),
            dma((8,)), dma((8,)),
            dma((16,)), dma((16,)),
        ],
        compiler_params=pltpu.CompilerParams(
            collective_id=0, has_side_effects=True, vmem_limit_bytes=60 * 1024 * 1024
        ),
    )(
        delta,
        alpha.reshape(16, 128),
        eddy,
        courant,
        tile_map,
        obs_rows.transpose(1, 0, 2),
        gate_beam.reshape(row),
        gate_index.reshape(row),
        gate_column.reshape(row),
        gate_live.reshape(row),
        obs_weight.reshape(256, 4, 128),
        obs_precision.reshape(row),
    )
    grad_delta, grad_alpha = pl.pallas_call(
        hand_on,
        out_shape=(
            jax.ShapeDtypeStruct((4, 16, 16, 128), f32),
            jax.ShapeDtypeStruct((4, 4, 128), f32),
        ),
        in_specs=[anywhere] * 2,
        out_specs=(anywhere, anywhere),
        scratch_shapes=[dma((2,))],
        compiler_params=pltpu.CompilerParams(vmem_limit_bytes=60 * 1024 * 1024),
    )(grad_delta, grad_alpha)
    return grad_delta, grad_alpha.reshape(1, 4, 4, 128)


def solution(mesh):
    return jax.shard_map(
        on_device,
        mesh=mesh,
        in_specs=(
            P(None, "gx", "gy", None),
            P("gx", "gy", None, None),
            P("gx", "gy", None),
            P(None, "gx", "gy", None),
            P("gx", "gy"),
            P(("gx", "gy"), None, None),
            P("gx", "gy", None),
            P("gx", "gy", None),
            P("gx", "gy", None),
            P("gx", "gy", None),
            P("gx", "gy", None, None, None),
            P("gx", "gy", None),
        ),
        out_specs=(P(None, "gx", "gy", None), P("gx", "gy", None, None)),
        check_vma=False,
    )
```

```python
import jax
import jax.numpy as jnp
from jax import lax
from jax.experimental import pallas as pl
from jax.experimental.pallas import tpu as pltpu
from jax.sharding import PartitionSpec as P

STEPS = 3
MESH = pl.DeviceIdType.MESH
f32 = jnp.float32
bf16 = jnp.bfloat16

X0, X1, XB = 4, 20, 24
Y0, Y1, YB = 8, 24, 32

DIRS = [(1, 0), (-1, 0), (0, 1), (0, -1), (1, 1), (1, -1), (-1, 1), (-1, -1)]


EDGES = (0, 1, 4, 5, 6, 7)
SIDES = (2, 3)


def inner_part(sign, lo, hi, width):
    if sign > 0:
        return pl.ds(hi - width, width)
    if sign < 0:
        return pl.ds(lo, width)
    return pl.ds(lo, hi - lo)


def outer_part(sign, lo, hi, width):
    if sign > 0:
        return pl.ds(hi, width)
    if sign < 0:
        return pl.ds(lo - width, width)
    return pl.ds(lo, hi - lo)


def split(value):
    high = value.astype(bf16)
    low = (value - high.astype(f32)).astype(bf16)
    return high, low


def dot(a, b):
    return jnp.dot(a, b, preferred_element_type=f32)


AT_ONCE = ((), (0,), (0, 1), (0, 1, 2), (0, 1, 2, 3, 5, 6), (0, 1, 2, 3, 4, 6, 7), (0, 1, 4, 5, 7), (0, 1, 2, 5, 6))
THROUGH = ((), (), (), (), ((5, 7),), (), ((5, 3), (4, 2)), ((6, 4), (5, 3)))
ANSWER = (
    ((1, (1,)), (2, (2,)), (7, (7, 6, 5)), (6, (4,)), (3, (3,))),
    ((2, (2,)), (3, (3,)), (7, (7, 6, 5)), (6, (4,))),
    ((3, (3,)), (4, (4, 5, 6)), (5, (7,))),
    ((4, (4, 6)), (5, (5, 7))),
    (), (), (), (),
)


def kernel(
    delta_h, alpha_h, eddy_h, courant_h, tmap_h, obs_h, beam_h, gidx_h, gcol_h, live_h, w_h, prec_h,
    out_d, out_a,
    dl, cf, k5, v0, v1, v2, v3, a1, a2, a3, wv, wc, w2, tm, ob, qi, vo, vi, gcol, glive, gprec,
    al, sums, rsums, rx, ry, rc,
    oh, sel, selt,
    lsem, asend, arecv, osend, orecv, qsend, qrecv, wsend, wrecv,
    csend, crecv, hsend, hrecv, psend, precv, ssend, srecv,
):
    nx = lax.axis_size("gx")
    ny = lax.axis_size("gy")
    nq = nx // 4
    ix = lax.axis_index("gx")
    iy = lax.axis_index("gy")
    iq = ix // 4
    im = ix % 4

    def there(d):
        dx, dy = DIRS[d]
        ok = None
        for sign, at, count in ((dx, ix, nx), (dy, iy, ny)):
            if sign > 0:
                cond = at < count - 1
            elif sign < 0:
                cond = at > 0
            else:
                continue
            ok = cond if ok is None else jnp.logical_and(ok, cond)
        return ok

    def peer(d):
        dx, dy = DIRS[d]
        return {"gx": ix + dx, "gy": iy + dy}

    barrier = pltpu.get_barrier_semaphore()

    def greet(gx, gy):
        pl.semaphore_signal(barrier, inc=1, device_id={"gx": gx, "gy": gy}, device_id_type=MESH)

    for t in range(16):

        @pl.when(t != iy)
        def _():
            greet(ix, t)

    greeted = 0
    for q in range(8):
        greeted = greeted + jnp.where(iq == q, len(AT_ONCE[q]), 0)
    expected = (ny - 1) + 3 + greeted
    for d in (0, 1, 4, 5, 6, 7):
        ok = there(d)

        @pl.when(ok)
        def _():
            greet(ix + DIRS[d][0], iy + DIRS[d][1])

        expected = expected + jnp.where(ok, 1, 0)
    for m in range(4):

        @pl.when(m != im)
        def _():
            greet(iq * 4 + m, iy)

    def far(table, act):
        for q in range(8):
            if table[q]:

                @pl.when(iq == q)
                def _():
                    for item in table[q]:
                        act(item)

    far([[r for r in range(8) if q in AT_ONCE[r]] for q in range(8)], lambda r: greet(r * 4 + im, iy))

    local = [
        pltpu.make_async_copy(alpha_h, al.at[iy], lsem.at[0]),
        pltpu.make_async_copy(obs_h, ob.at[iq], lsem.at[1]),
        pltpu.make_async_copy(eddy_h, cf.at[0, X0:X1, Y0:Y1], lsem.at[2]),
        pltpu.make_async_copy(courant_h, cf.at[pl.ds(1, 2), X0:X1, Y0:Y1], lsem.at[3]),
        pltpu.make_async_copy(beam_h, qi.at[im, pl.ds(0, 1)], lsem.at[4]),
        pltpu.make_async_copy(gidx_h, qi.at[im, pl.ds(1, 1)], lsem.at[5]),
        pltpu.make_async_copy(tmap_h, tm, lsem.at[6]),
        pltpu.make_async_copy(gcol_h, gcol, lsem.at[7]),
        pltpu.make_async_copy(live_h, glive, lsem.at[8]),
        pltpu.make_async_copy(prec_h, gprec, lsem.at[9]),
        pltpu.make_async_copy(w_h, wv, lsem.at[10]),
        pltpu.make_async_copy(delta_h, dl, lsem.at[11]),
    ]
    for copy in local:
        copy.start()

    def remote(src, dst, send, recv, gx, gy):
        return pltpu.make_async_remote_copy(
            src_ref=src,
            dst_ref=dst,
            send_sem=send,
            recv_sem=recv,
            device_id={"gx": gx, "gy": gy},
            device_id_type=MESH,
        )

    def alpha_out(t):
        return remote(al.at[iy], al.at[iy], asend.at[t], arecv.at[iy], ix, t)

    def alpha_in(t):
        return remote(al.at[t], al.at[t], asend.at[t], arecv.at[t], ix, t)

    def obs_out(q):
        return remote(ob.at[iq], ob.at[iq], osend.at[q], orecv.at[iq], q * 4 + im, iy)

    def obs_in(q):
        return remote(ob.at[q], ob.at[q], osend.at[q], orecv.at[q], q * 4 + im, iy)

    def index_out(m):
        return remote(qi.at[im], qi.at[im], qsend.at[m], qrecv.at[im], iq * 4 + m, iy)

    def index_in(m):
        return remote(qi.at[m], qi.at[m], qsend.at[m], qrecv.at[m], iq * 4 + m, iy)

    def value_out(m):
        return remote(vo.at[m], vi.at[im], wsend.at[m], wrecv.at[im], iq * 4 + m, iy)

    def value_in(m):
        return remote(vo.at[m], vi.at[m], wsend.at[m], wrecv.at[m], iq * 4 + m, iy)

    def sums_out(t):
        return remote(sums.at[t], rsums.at[iy], ssend.at[t], srecv.at[iy], ix, t)

    def sums_in(t):
        return remote(sums.at[t], rsums.at[t], ssend.at[t], srecv.at[t], ix, t)

    def among(count, where, act):
        for t in range(count):

            @pl.when(where(t))
            def _():
                act(t)

    ox = (iy // 2) % 4
    others = []
    for dy, dx in ((1, 2), (1, 1), (1, 3), (0, 2), (1, 0), (0, 1), (0, 3), (0, 0)):
        for dc in (1, 0):
            if (dy, dx, dc) != (0, 0, 0):
                ty = (iy // 8 + dy) % 2
                others.append(ty * 8 + ((ox + dx) % 4) * 2 + (iy + dc) % 2)

    def strip(act):
        for t in others:
            act(t)

    def not_m(m):
        return m != im

    local[0].wait()
    local[1].wait()
    pl.semaphore_wait(barrier, expected)
    strip(lambda t: alpha_out(t).start())
    far(AT_ONCE, lambda q: obs_out(q).start())

    def halo_copy(ref, d, width, sends, receives):
        dx, dy = DIRS[d]
        if dx != 0 and dy != 0:
            width = width - 1
        gx, gy = ix + dx, iy + dy
        return remote(
            ref.at[:, inner_part(dx, X0, X1, width), inner_part(dy, Y0, Y1, width)],
            ref.at[:, outer_part(-dx, X0, X1, width), outer_part(-dy, Y0, Y1, width)],
            sends.at[d],
            receives.at[d],
            gx,
            gy,
        )

    def each(make, act, back, those=range(8)):
        for d in those:
            dx, dy = DIRS[d]
            here = DIRS.index((-dx, -dy)) if back else d

            @pl.when(there(here))
            def _():
                act(make(d))

    def start(copy):
        copy.start()

    def wait_send(copy):
        copy.wait_send()

    def wait_recv(copy):
        copy.wait_recv()

    def coef_copy(d):
        return halo_copy(cf, d, 2, csend, crecv)

    def state_copy(d):
        return halo_copy(v0, d, 3, hsend, hrecv)

    local[2].wait()
    local[3].wait()
    each(coef_copy, start, False)
    local[4].wait()
    local[5].wait()
    among(4, not_m, lambda m: index_out(m).start())

    def zero(ref, x, y):
        ref[:, x[0] : x[1], y[0] : y[1]] = jnp.zeros((ref.shape[0], x[1] - x[0], y[1] - y[0], 128), f32)

    def missing(ref, width):
        for d, (dx, dy) in enumerate(DIRS):
            wide = width - 1 if dx != 0 and dy != 0 else width
            spans = []
            for sign, lo, hi in ((dx, X0, X1), (dy, Y0, Y1)):
                spans.append((hi, hi + wide) if sign > 0 else (lo - wide, lo) if sign < 0 else (lo, hi))

            @pl.when(jnp.logical_not(there(d)))
            def _():
                zero(ref, *spans)

    missing(cf, 2)
    missing(v0, 3)
    zero(cf, (0, 2), (0, YB))
    zero(cf, (22, XB), (0, YB))
    zero(cf, (2, 22), (0, 6))
    zero(cf, (2, 22), (26, YB))
    for x in (2, 21):
        zero(cf, (x, x + 1), (6, 8))
        zero(cf, (x, x + 1), (24, 26))
    for x in (3, 20):
        zero(cf, (x, x + 1), (6, 7))
        zero(cf, (x, x + 1), (25, 26))

    local[6].wait()
    lane = lax.broadcasted_iota(jnp.int32, (256, 128), 1)
    row = lax.broadcasted_iota(jnp.int32, (256, 128), 0)
    lanes = lane.astype(f32)
    up = lax.broadcasted_iota(jnp.int32, (256, 256), 0).astype(f32)
    of_row = jnp.where(row // 16 == lane, 1.0, 0.0).astype(bf16)
    tiles = jnp.concatenate(
        [
            jnp.concatenate([tm[...].astype(f32), jnp.zeros((16, 112), f32)], axis=1),
            jnp.zeros((112, 128), f32),
        ],
        axis=0,
    ).astype(bf16)
    picked = jnp.where(row % 16 == lane, dot(of_row, tiles), 0.0).astype(bf16)
    tile_at = dot(picked, jnp.ones((128, 128), bf16)) * 4.0

    def hot(values):
        return jnp.concatenate(
            [jnp.where(values == lanes, 1.0, 0.0), jnp.where(values == lanes + 128.0, 1.0, 0.0)], axis=1
        ).astype(bf16)

    for c in range(4):
        sel[c * 256 : (c + 1) * 256] = hot(tile_at + float(c))
    tile_row = tile_at.T[0:1]
    for c in range(4):
        selt[:, c * 256 : (c + 1) * 256] = jnp.where(up == tile_row + float(c), 1.0, 0.0).astype(bf16)
    for copy in local[7:12]:
        copy.wait()

    slot_column = gcol[0:1].astype(f32)
    at_slot = jnp.where(up == slot_column, 1.0, 0.0).T.astype(bf16)
    oh[:, :256] = at_slot
    oh[:, 256:] = at_slot
    for c in range(4):
        weight = wv[:, c, :]
        high, low = split(weight)
        wc[c] = weight
        w2[0:256, c * 128 : (c + 1) * 128] = high
        w2[256:512, c * 128 : (c + 1) * 128] = low
        w2[512:768, c * 128 : (c + 1) * 128] = high
    rx_rows = ((0, 3), (3, 6))
    for d, x in ((0, rx_rows[1]), (1, rx_rows[0])):

        @pl.when(jnp.logical_not(there(d)))
        def _():
            zero(rx, x, (0, 16))

    zero(ry, (0, 16), (3, 13))
    for d, y in ((2, (13, 16)), (3, (0, 3))):

        @pl.when(jnp.logical_not(there(d)))
        def _():
            zero(ry, (0, 16), y)

    zero(rc, (0, 4), (2, 14))
    for d in (4, 5, 6, 7):
        dx, dy = DIRS[d]

        @pl.when(jnp.logical_not(there(d)))
        def _():
            zero(rc, (2, 4) if dx > 0 else (0, 2), (14, 16) if dy > 0 else (0, 2))

    for ref in (a1, a2, a3):
        zero(ref, (0, X0), (0, YB))
        zero(ref, (X1, XB), (0, YB))
        zero(ref, (X0, X1), (0, Y0))
        zero(ref, (X0, X1), (Y1, YB))

    def through(item):
        obs_in(item[0]).wait_recv()
        obs_out(item[1]).start()

    far(THROUGH, through)

    strip(lambda t: alpha_in(t).wait_recv())
    high, low = split(al[...].reshape(256, 128))
    both = jnp.concatenate([high, low], axis=1)

    def state_rows(x0, x1):
        for c in range(4):
            product = dot(sel[c * 256 + x0 * 16 : c * 256 + x1 * 16], both)
            profile = (product[:, :128] + product[:, 128:]).reshape(x1 - x0, 16, 128)
            v0[c, X0 + x0 : X0 + x1, Y0:Y1] = dl[c, x0:x1] + 0.125 * profile

    state_rows(0, 3)
    state_rows(13, 16)
    each(state_copy, start, False, EDGES)
    state_rows(3, 13)
    each(state_copy, start, False, SIDES)

    def answer(item):
        obs_in(item[0]).wait_recv()
        for q in item[1]:
            obs_out(q).start()

    far([ANSWER[q] if q >= 2 else () for q in range(8)], answer)

    each(coef_copy, wait_recv, True)

    def derive(x, carry):
        e = cf[0, x]
        half_x = 0.5 * cf[1, x]
        half_y = 0.5 * cf[2, x]
        k5[0, x] = 1.0 - 4.0 * e
        k5[1, x] = e - half_x
        k5[2, x] = e + half_x
        k5[3, x] = e - half_y
        k5[4, x] = e + half_y
        return carry

    lax.fori_loop(0, XB, derive, 0)

    far([ANSWER[q] if q < 2 else () for q in range(8)], answer)
    among(4, not_m, lambda m: index_in(m).wait_recv())
    waited = [[t for t, _ in THROUGH[q] + ANSWER[q]] + [q] for q in range(8)]
    far([[r for r in range(8) if r not in waited[q]] for q in range(8)], lambda q: obs_in(q).wait_recv())
    turned = [split(ob[:, step].reshape(64, 128).T) for step in range(STEPS)]
    table = jnp.concatenate([jnp.concatenate(pair, axis=1) for pair in turned], axis=0)
    down64 = lax.broadcasted_iota(jnp.int32, (64, 256), 0)
    down128 = lax.broadcasted_iota(jnp.int32, (128, 256), 0)
    for m in range(4):
        beams = qi[m, 0:1]
        held = jnp.where((beams // 8) % 4 == im, (beams // 32) * 8 + beams % 8, -1)
        at_beam = jnp.where(down64 == held, 1.0, 0.0).astype(bf16)
        found = dot(table, jnp.concatenate([at_beam, at_beam], axis=0))
        at_gate = down128 == qi[m, 1:2]
        for step in range(STEPS):
            both = found[step * 128 : (step + 1) * 128]
            vo[m, step : step + 1] = jnp.sum(jnp.where(at_gate, both, 0.0), axis=0, keepdims=True)
    among(4, not_m, lambda m: value_out(m).start())

    each(state_copy, wait_recv, True)

    def forward(src, dst, margin):
        y0, rows = (Y0, 16) if margin == 0 else (4, 24)

        def body(x, carry):
            mid = pl.ds(y0, rows)
            dst[:, x, mid] = (
                k5[0, x, mid] * src[:, x, mid]
                + k5[1, x, mid] * src[:, x + 1, mid]
                + k5[2, x, mid] * src[:, x - 1, mid]
                + k5[3, x, mid] * src[:, x, pl.ds(y0 + 1, rows)]
                + k5[4, x, mid] * src[:, x, pl.ds(y0 - 1, rows)]
            )
            return carry

        lax.fori_loop(X0 - margin, X1 + margin, body, 0)

    def backward(src, dst, first, last, extra):
        y0, rows = 4, 24

        def body(x, carry):
            mid = pl.ds(y0, rows)
            below = pl.ds(y0 - 1, rows)
            above = pl.ds(y0 + 1, rows)
            dst[:, x, mid] = (
                k5[0, x, mid] * src[:, x, mid]
                + k5[1, x - 1, mid] * src[:, x - 1, mid]
                + k5[2, x + 1, mid] * src[:, x + 1, mid]
                + k5[3, x, below] * src[:, x, below]
                + k5[4, x, above] * src[:, x, above]
            )
            return carry

        lax.fori_loop(first, last, body, 0)
        if extra is not None:
            for c in range(4):
                dst[c, X0:X1, Y0:Y1] += extra[c]

    ones = jnp.ones((8, 128), bf16)

    def along(value):
        return lax.dot_general(ones, value, (((1,), (1,)), ((), ())), preferred_element_type=f32)[0:1]

    def looked(state):
        parts = [split(state[c, X0:X1, Y0:Y1].reshape(256, 128)) for c in range(4)]
        halves = [jnp.concatenate([part[k] for part in parts], axis=1) for k in range(2)]
        product = dot(oh[...], jnp.concatenate(halves, axis=0))
        total = None
        for c in range(4):
            term = product[:, c * 128 : (c + 1) * 128] * wc[c]
            total = term if total is None else total + term
        high, low = split(total)
        return along(high) + along(low)

    forward(v0, v1, 2)
    seen = [looked(v1)]
    forward(v1, v2, 1)
    seen.append(looked(v2))
    forward(v2, v3, 0)
    seen.append(looked(v3))

    among(4, not_m, lambda m: value_in(m).wait_recv())
    vi[im] = vo[im]
    scale = glive[...].astype(f32) * gprec[...]
    mask = up == slot_column

    def forcing(step):
        observed = vi[0, step : step + 1] + vi[1, step : step + 1] + vi[2, step : step + 1] + vi[3, step : step + 1]
        misfit = scale * (seen[step] - observed)
        coarse = misfit.astype(bf16).astype(f32)
        fine = misfit - coarse
        high = jnp.where(mask, coarse, 0.0).astype(bf16)
        low = jnp.where(mask, fine, 0.0).astype(bf16)
        product = dot(jnp.concatenate([high, high, low], axis=1), w2[...])
        return [product[:, c * 128 : (c + 1) * 128].reshape(16, 16, 128) for c in range(4)]

    last = forcing(2)
    for c in range(4):
        a3[c, X0:X1, Y0:Y1] = last[c]
    backward(a3, a2, X0 - 1, X1 + 1, forcing(1))
    backward(a2, a1, X0 - 2, X1 + 2, forcing(0))
    backward(a1, v1, X0 - 3, X0, None)
    backward(a1, v1, X1, X1 + 3, None)

    def push_copy(d):
        dx, dy = DIRS[d]
        width = 2 if dx != 0 and dy != 0 else 3
        src = v1.at[:, outer_part(dx, X0, X1, width), outer_part(dy, Y0, Y1, width)]
        at_y = inner_part(-dy, 0, 16, width)
        if dy == 0:
            dst = rx.at[:, inner_part(-dx, 0, 6, width)]
        elif dx == 0:
            dst = ry.at[:, :, at_y]
        else:
            dst = rc.at[:, inner_part(-dx, 0, 4, width), at_y]
        return remote(src, dst, psend.at[d], precv.at[d], ix + dx, iy + dy)

    each(push_copy, start, False, EDGES)
    backward(a1, v1, X0, X1, None)
    each(push_copy, start, False, SIDES)
    each(push_copy, wait_recv, True)
    total = None
    for c in range(4):
        v3[c, X0:X1, Y0:Y1] = v1[c, X0:X1, Y0:Y1] + ry[c]
        v3[c, X0 : X0 + 3, Y0:Y1] += rx[c, 0:3]
        v3[c, X1 - 3 : X1, Y0:Y1] += rx[c, 3:6]
        v3[c, X0 : X0 + 2, Y0:Y1] += rc[c, 0:2]
        v3[c, X1 - 2 : X1, Y0:Y1] += rc[c, 2:4]
        high, low = split(v3[c, X0:X1, Y0:Y1].reshape(256, 128))
        product = dot(selt[:, c * 256 : (c + 1) * 256], jnp.concatenate([high, low], axis=1))
        term = product[:, :128] + product[:, 128:]
        total = term if total is None else total + term
    sums[...] = total.reshape(16, 16, 128)
    strip(lambda t: sums_out(t).start())
    rsums[iy] = sums[iy]
    for c in range(4):
        out_d[c] = dl[c] + v3[c, X0:X1, Y0:Y1]
    strip(lambda t: alpha_out(t).wait_send())
    among(8, lambda q: q != iq, lambda q: obs_out(q).wait_send())
    among(4, not_m, lambda m: index_out(m).wait_send())
    among(4, not_m, lambda m: value_out(m).wait_send())
    each(coef_copy, wait_send, False)
    each(state_copy, wait_send, False)
    each(push_copy, wait_send, False)
    strip(lambda t: sums_in(t).wait_recv())
    result = al[iy] + 0.125 * jnp.sum(rsums[...], axis=0)
    for t in range(4):
        out_a[t] = result[4 * t : 4 * t + 4]
    strip(lambda t: sums_out(t).wait_send())


def on_device(
    delta, alpha, eddy, courant, tile_map, obs_rows,
    gate_beam, gate_index, gate_column, gate_live, obs_weight, obs_precision,
):
    dma = pltpu.SemaphoreType.DMA
    vm = pltpu.VMEM
    frame = vm((4, XB, YB, 128), f32)
    slots = vm((1, 256), jnp.int32)
    anywhere = pl.BlockSpec(memory_space=pl.ANY)
    inside = pl.BlockSpec(memory_space=pltpu.VMEM)
    row = (1, 256)
    grad_delta, grad_alpha = pl.pallas_call(
        kernel,
        out_shape=(vm((4, 16, 16, 128), f32), vm((4, 4, 128), f32)),
        in_specs=[anywhere] * 12,
        out_specs=(inside, inside),
        scratch_shapes=[
            vm((4, 16, 16, 128), f32),
            vm((3, XB, YB, 128), f32),
            vm((5, XB, YB, 128), f32),
            frame, frame, frame, frame,
            frame, frame, frame,
            vm((256, 4, 128), f32),
            vm((4, 256, 128), f32),
            vm((768, 512), bf16),
            vm((16, 16), jnp.int32),
            vm((8, 3, 8, 128), f32),
            vm((4, 2, 256), jnp.int32),
            vm((4, 3, 256), f32),
            vm((4, 3, 256), f32),
            slots, slots,
            vm((1, 256), f32),
            vm((16, 16, 128), f32),
            vm((16, 16, 128), f32),
            vm((16, 16, 128), f32),
            vm((4, 6, 16, 128), f32),
            vm((4, 16, 16, 128), f32),
            vm((4, 4, 16, 128), f32),
            vm((256, 512), bf16),
            vm((1024, 256), bf16),
            vm((256, 1024), bf16),
            dma((12,)),
            dma((16,)), dma((16,)),
            dma((8,)), dma((8,)),
            dma((4,)), dma((4,)),
            dma((4,)), dma((4,)),
            dma((8,)), dma((8,)),
            dma((8,)), dma((8,)),
            dma((8,)), dma((8,)),
            dma((16,)), dma((16,)),
        ],
        compiler_params=pltpu.CompilerParams(
            collective_id=0, has_side_effects=True, vmem_limit_bytes=60 * 1024 * 1024
        ),
    )(
        delta,
        alpha.reshape(16, 128),
        eddy,
        courant,
        tile_map,
        obs_rows.transpose(1, 0, 2),
        gate_beam.reshape(row),
        gate_index.reshape(row),
        gate_column.reshape(row),
        gate_live.reshape(row),
        obs_weight.reshape(256, 4, 128),
        obs_precision.reshape(row),
    )
    return grad_delta, grad_alpha.reshape(1, 4, 4, 128)


def solution(mesh):
    return jax.shard_map(
        on_device,
        mesh=mesh,
        in_specs=(
            P(None, "gx", "gy", None),
            P("gx", "gy", None, None),
            P("gx", "gy", None),
            P(None, "gx", "gy", None),
            P("gx", "gy"),
            P(("gx", "gy"), None, None),
            P("gx", "gy", None),
            P("gx", "gy", None),
            P("gx", "gy", None),
            P("gx", "gy", None),
            P("gx", "gy", None, None, None),
            P("gx", "gy", None),
        ),
        out_specs=(P(None, "gx", "gy", None), P("gx", "gy", None, None)),
        check_vma=False,
    )
```

```python
import jax
import jax.numpy as jnp
from jax import lax
from jax.experimental import pallas as pl
from jax.experimental.pallas import tpu as pltpu
from jax.sharding import PartitionSpec as P

STEPS = 3
MESH = pl.DeviceIdType.MESH
f32 = jnp.float32
bf16 = jnp.bfloat16

X0, X1, XB = 4, 20, 24
Y0, Y1, YB = 8, 24, 32

DIRS = [(1, 0), (-1, 0), (0, 1), (0, -1), (1, 1), (1, -1), (-1, 1), (-1, -1)]


EDGES = (0, 1, 4, 5, 6, 7)
SIDES = (2, 3)


def inner_part(sign, lo, hi, width):
    if sign > 0:
        return pl.ds(hi - width, width)
    if sign < 0:
        return pl.ds(lo, width)
    return pl.ds(lo, hi - lo)


def outer_part(sign, lo, hi, width):
    if sign > 0:
        return pl.ds(hi, width)
    if sign < 0:
        return pl.ds(lo - width, width)
    return pl.ds(lo, hi - lo)


def split(value):
    high = value.astype(bf16)
    low = (value - high.astype(f32)).astype(bf16)
    return high, low


def dot(a, b):
    return jnp.dot(a, b, preferred_element_type=f32)


AT_ONCE = ((), (0,), (0, 1), (0, 1, 2), (0, 1, 2, 3, 5, 6), (0, 1, 2, 3, 4, 6, 7), (0, 1, 2, 3, 4, 5, 7), (0, 1, 2, 3, 5, 6))
THROUGH = ((), (), (), (), ((5, 7),), (), (), ((6, 4),))
ANSWER = (
    ((1, (1,)), (2, (2,)), (7, (7, 6, 5)), (6, (4,)), (3, (3,))),
    ((2, (2,)), (3, (3,)), (7, (7, 6, 5)), (6, (4,))),
    ((3, (3,)), (4, (4, 5, 6)), (5, (7,))),
    ((4, (4, 6)), (5, (5, 7))),
    (), (), (), (),
)


def kernel(
    delta_h, alpha_h, eddy_h, courant_h, tmap_h, obs_h, beam_h, gidx_h, gcol_h, live_h, w_h, prec_h,
    out_d, out_a,
    dl, cf, k5, v0, v1, v2, v3, a1, a2, a3, wv, wc, w2, tm, ob, qi, vo, vi, gcol, glive, gprec,
    al, sums, rsums, rx, ry, rc,
    oh, sel, selt,
    lsem, asend, arecv, osend, orecv, qsend, qrecv, wsend, wrecv,
    csend, crecv, hsend, hrecv, psend, precv, ssend, srecv,
):
    nx = lax.axis_size("gx")
    ny = lax.axis_size("gy")
    nq = nx // 4
    ix = lax.axis_index("gx")
    iy = lax.axis_index("gy")
    iq = ix // 4
    im = ix % 4

    def there(d):
        dx, dy = DIRS[d]
        ok = None
        for sign, at, count in ((dx, ix, nx), (dy, iy, ny)):
            if sign > 0:
                cond = at < count - 1
            elif sign < 0:
                cond = at > 0
            else:
                continue
            ok = cond if ok is None else jnp.logical_and(ok, cond)
        return ok

    def peer(d):
        dx, dy = DIRS[d]
        return {"gx": ix + dx, "gy": iy + dy}

    barrier = pltpu.get_barrier_semaphore()

    def greet(gx, gy):
        pl.semaphore_signal(barrier, inc=1, device_id={"gx": gx, "gy": gy}, device_id_type=MESH)

    def far(table, act):
        for q in range(8):
            if table[q]:

                @pl.when(iq == q)
                def _():
                    for item in table[q]:
                        act(item)

    far([[r for r in range(8) if q in AT_ONCE[r]] for q in range(8)], lambda r: greet(r * 4 + im, iy))

    for t in range(16):

        @pl.when(t != iy)
        def _():
            greet(ix, t)

    greeted = 0
    for q in range(8):
        greeted = greeted + jnp.where(iq == q, len(AT_ONCE[q]), 0)
    expected = (ny - 1) + 3 + greeted
    for d in (0, 1, 4, 5, 6, 7):
        ok = there(d)

        @pl.when(ok)
        def _():
            greet(ix + DIRS[d][0], iy + DIRS[d][1])

        expected = expected + jnp.where(ok, 1, 0)
    for m in range(4):

        @pl.when(m != im)
        def _():
            greet(iq * 4 + m, iy)

    local = [
        pltpu.make_async_copy(alpha_h, al.at[iy], lsem.at[0]),
        pltpu.make_async_copy(obs_h, ob.at[iq], lsem.at[1]),
        pltpu.make_async_copy(eddy_h, cf.at[0, X0:X1, Y0:Y1], lsem.at[2]),
        pltpu.make_async_copy(courant_h, cf.at[pl.ds(1, 2), X0:X1, Y0:Y1], lsem.at[3]),
        pltpu.make_async_copy(beam_h, qi.at[im, pl.ds(0, 1)], lsem.at[4]),
        pltpu.make_async_copy(gidx_h, qi.at[im, pl.ds(1, 1)], lsem.at[5]),
        pltpu.make_async_copy(tmap_h, tm, lsem.at[6]),
        pltpu.make_async_copy(gcol_h, gcol, lsem.at[7]),
        pltpu.make_async_copy(live_h, glive, lsem.at[8]),
        pltpu.make_async_copy(prec_h, gprec, lsem.at[9]),
        pltpu.make_async_copy(w_h, wv, lsem.at[10]),
        pltpu.make_async_copy(delta_h, dl, lsem.at[11]),
    ]
    for copy in local:
        copy.start()

    def remote(src, dst, send, recv, gx, gy):
        return pltpu.make_async_remote_copy(
            src_ref=src,
            dst_ref=dst,
            send_sem=send,
            recv_sem=recv,
            device_id={"gx": gx, "gy": gy},
            device_id_type=MESH,
        )

    def alpha_out(t):
        return remote(al.at[iy], al.at[iy], asend.at[t], arecv.at[iy], ix, t)

    def alpha_in(t):
        return remote(al.at[t], al.at[t], asend.at[t], arecv.at[t], ix, t)

    def obs_out(q):
        return remote(ob.at[iq], ob.at[iq], osend.at[q], orecv.at[iq], q * 4 + im, iy)

    def obs_in(q):
        return remote(ob.at[q], ob.at[q], osend.at[q], orecv.at[q], q * 4 + im, iy)

    def index_out(m):
        return remote(qi.at[im], qi.at[im], qsend.at[m], qrecv.at[im], iq * 4 + m, iy)

    def index_in(m):
        return remote(qi.at[m], qi.at[m], qsend.at[m], qrecv.at[m], iq * 4 + m, iy)

    def value_out(m):
        return remote(vo.at[m], vi.at[im], wsend.at[m], wrecv.at[im], iq * 4 + m, iy)

    def value_in(m):
        return remote(vo.at[m], vi.at[m], wsend.at[m], wrecv.at[m], iq * 4 + m, iy)

    def sums_out(t):
        return remote(sums.at[t], rsums.at[iy], ssend.at[t], srecv.at[iy], ix, t)

    def sums_in(t):
        return remote(sums.at[t], rsums.at[t], ssend.at[t], srecv.at[t], ix, t)

    def among(count, where, act):
        for t in range(count):

            @pl.when(where(t))
            def _():
                act(t)

    ox = (iy // 2) % 4
    others = []
    for dy, dx in ((1, 2), (1, 1), (1, 3), (0, 2), (1, 0), (0, 1), (0, 3), (0, 0)):
        for dc in (1, 0):
            if (dy, dx, dc) != (0, 0, 0):
                ty = (iy // 8 + dy) % 2
                others.append(ty * 8 + ((ox + dx) % 4) * 2 + (iy + dc) % 2)

    def strip(act):
        for t in others:
            act(t)

    def not_m(m):
        return m != im

    local[0].wait()
    local[1].wait()
    pl.semaphore_wait(barrier, expected)
    far(AT_ONCE, lambda q: obs_out(q).start())
    strip(lambda t: alpha_out(t).start())

    def halo_copy(ref, d, width, sends, receives):
        dx, dy = DIRS[d]
        if dx != 0 and dy != 0:
            width = width - 1
        gx, gy = ix + dx, iy + dy
        return remote(
            ref.at[:, inner_part(dx, X0, X1, width), inner_part(dy, Y0, Y1, width)],
            ref.at[:, outer_part(-dx, X0, X1, width), outer_part(-dy, Y0, Y1, width)],
            sends.at[d],
            receives.at[d],
            gx,
            gy,
        )

    def each(make, act, back, those=range(8)):
        for d in those:
            dx, dy = DIRS[d]
            here = DIRS.index((-dx, -dy)) if back else d

            @pl.when(there(here))
            def _():
                act(make(d))

    def start(copy):
        copy.start()

    def wait_send(copy):
        copy.wait_send()

    def wait_recv(copy):
        copy.wait_recv()

    def coef_copy(d):
        return halo_copy(cf, d, 2, csend, crecv)

    def state_copy(d):
        return halo_copy(v0, d, 3, hsend, hrecv)

    local[2].wait()
    local[3].wait()
    each(coef_copy, start, False)
    local[4].wait()
    local[5].wait()
    among(4, not_m, lambda m: index_out(m).start())

    def zero(ref, x, y):
        ref[:, x[0] : x[1], y[0] : y[1]] = jnp.zeros((ref.shape[0], x[1] - x[0], y[1] - y[0], 128), f32)

    def missing(ref, width):
        for d, (dx, dy) in enumerate(DIRS):
            wide = width - 1 if dx != 0 and dy != 0 else width
            spans = []
            for sign, lo, hi in ((dx, X0, X1), (dy, Y0, Y1)):
                spans.append((hi, hi + wide) if sign > 0 else (lo - wide, lo) if sign < 0 else (lo, hi))

            @pl.when(jnp.logical_not(there(d)))
            def _():
                zero(ref, *spans)

    missing(cf, 2)
    missing(v0, 3)
    zero(cf, (0, 2), (0, YB))
    zero(cf, (22, XB), (0, YB))
    zero(cf, (2, 22), (0, 6))
    zero(cf, (2, 22), (26, YB))
    for x in (2, 21):
        zero(cf, (x, x + 1), (6, 8))
        zero(cf, (x, x + 1), (24, 26))
    for x in (3, 20):
        zero(cf, (x, x + 1), (6, 7))
        zero(cf, (x, x + 1), (25, 26))

    local[6].wait()
    lane = lax.broadcasted_iota(jnp.int32, (256, 128), 1)
    row = lax.broadcasted_iota(jnp.int32, (256, 128), 0)
    lanes = lane.astype(f32)
    up = lax.broadcasted_iota(jnp.int32, (256, 256), 0).astype(f32)
    of_row = jnp.where(row // 16 == lane, 1.0, 0.0).astype(bf16)
    tiles = jnp.concatenate(
        [
            jnp.concatenate([tm[...].astype(f32), jnp.zeros((16, 112), f32)], axis=1),
            jnp.zeros((112, 128), f32),
        ],
        axis=0,
    ).astype(bf16)
    picked = jnp.where(row % 16 == lane, dot(of_row, tiles), 0.0).astype(bf16)
    tile_at = dot(picked, jnp.ones((128, 128), bf16)) * 4.0

    def hot(values):
        return jnp.concatenate(
            [jnp.where(values == lanes, 1.0, 0.0), jnp.where(values == lanes + 128.0, 1.0, 0.0)], axis=1
        ).astype(bf16)

    for c in range(4):
        sel[c * 256 : (c + 1) * 256] = hot(tile_at + float(c))
    tile_row = tile_at.T[0:1]
    for c in range(4):
        selt[:, c * 256 : (c + 1) * 256] = jnp.where(up == tile_row + float(c), 1.0, 0.0).astype(bf16)
    for copy in local[7:12]:
        copy.wait()

    slot_column = gcol[0:1].astype(f32)
    at_slot = jnp.where(up == slot_column, 1.0, 0.0).T.astype(bf16)
    oh[:, :256] = at_slot
    oh[:, 256:] = at_slot
    for c in range(4):
        weight = wv[:, c, :]
        high, low = split(weight)
        wc[c] = weight
        w2[0:256, c * 128 : (c + 1) * 128] = high
        w2[256:512, c * 128 : (c + 1) * 128] = low
        w2[512:768, c * 128 : (c + 1) * 128] = high
    rx_rows = ((0, 3), (3, 6))
    for d, x in ((0, rx_rows[1]), (1, rx_rows[0])):

        @pl.when(jnp.logical_not(there(d)))
        def _():
            zero(rx, x, (0, 16))

    zero(ry, (0, 16), (3, 13))
    for d, y in ((2, (13, 16)), (3, (0, 3))):

        @pl.when(jnp.logical_not(there(d)))
        def _():
            zero(ry, (0, 16), y)

    zero(rc, (0, 4), (2, 14))
    for d in (4, 5, 6, 7):
        dx, dy = DIRS[d]

        @pl.when(jnp.logical_not(there(d)))
        def _():
            zero(rc, (2, 4) if dx > 0 else (0, 2), (14, 16) if dy > 0 else (0, 2))

    for ref in (a1, a2, a3):
        zero(ref, (0, X0), (0, YB))
        zero(ref, (X1, XB), (0, YB))
        zero(ref, (X0, X1), (0, Y0))
        zero(ref, (X0, X1), (Y1, YB))

    def through(item):
        obs_in(item[0]).wait_recv()
        obs_out(item[1]).start()

    far(THROUGH, through)

    strip(lambda t: alpha_in(t).wait_recv())
    high, low = split(al[...].reshape(256, 128))
    both = jnp.concatenate([high, low], axis=1)

    def state_rows(x0, x1):
        for c in range(4):
            product = dot(sel[c * 256 + x0 * 16 : c * 256 + x1 * 16], both)
            profile = (product[:, :128] + product[:, 128:]).reshape(x1 - x0, 16, 128)
            v0[c, X0 + x0 : X0 + x1, Y0:Y1] = dl[c, x0:x1] + 0.125 * profile

    state_rows(0, 3)
    state_rows(13, 16)
    each(state_copy, start, False, EDGES)
    state_rows(3, 13)
    each(state_copy, start, False, SIDES)

    def answer(item):
        obs_in(item[0]).wait_recv()
        for q in item[1]:
            obs_out(q).start()

    far([ANSWER[q] if q >= 2 else () for q in range(8)], answer)

    each(coef_copy, wait_recv, True)

    def derive(x, carry):
        e = cf[0, x]
        half_x = 0.5 * cf[1, x]
        half_y = 0.5 * cf[2, x]
        k5[0, x] = 1.0 - 4.0 * e
        k5[1, x] = e - half_x
        k5[2, x] = e + half_x
        k5[3, x] = e - half_y
        k5[4, x] = e + half_y
        return carry

    lax.fori_loop(0, XB, derive, 0)

    far([ANSWER[q] if q < 2 else () for q in range(8)], answer)
    among(4, not_m, lambda m: index_in(m).wait_recv())
    waited = [[t for t, _ in THROUGH[q] + ANSWER[q]] + [q] for q in range(8)]
    far([[r for r in range(8) if r not in waited[q]] for q in range(8)], lambda q: obs_in(q).wait_recv())
    turned = [split(ob[:, step].reshape(64, 128).T) for step in range(STEPS)]
    table = jnp.concatenate([jnp.concatenate(pair, axis=1) for pair in turned], axis=0)
    down64 = lax.broadcasted_iota(jnp.int32, (64, 256), 0)
    down128 = lax.broadcasted_iota(jnp.int32, (128, 256), 0)
    for m in range(4):
        beams = qi[m, 0:1]
        held = jnp.where((beams // 8) % 4 == im, (beams // 32) * 8 + beams % 8, -1)
        at_beam = jnp.where(down64 == held, 1.0, 0.0).astype(bf16)
        found = dot(table, jnp.concatenate([at_beam, at_beam], axis=0))
        at_gate = down128 == qi[m, 1:2]
        for step in range(STEPS):
            both = found[step * 128 : (step + 1) * 128]
            vo[m, step : step + 1] = jnp.sum(jnp.where(at_gate, both, 0.0), axis=0, keepdims=True)

        @pl.when(m != im)
        def _():
            value_out(m).start()


    each(state_copy, wait_recv, True)

    def forward(src, dst, margin):
        y0, rows = (Y0, 16) if margin == 0 else (4, 24)

        def body(x, carry):
            mid = pl.ds(y0, rows)
            dst[:, x, mid] = (
                k5[0, x, mid] * src[:, x, mid]
                + k5[1, x, mid] * src[:, x + 1, mid]
                + k5[2, x, mid] * src[:, x - 1, mid]
                + k5[3, x, mid] * src[:, x, pl.ds(y0 + 1, rows)]
                + k5[4, x, mid] * src[:, x, pl.ds(y0 - 1, rows)]
            )
            return carry

        lax.fori_loop(X0 - margin, X1 + margin, body, 0)

    def backward(src, dst, first, last, extra):
        y0, rows = 4, 24

        def body(x, carry):
            mid = pl.ds(y0, rows)
            below = pl.ds(y0 - 1, rows)
            above = pl.ds(y0 + 1, rows)
            dst[:, x, mid] = (
                k5[0, x, mid] * src[:, x, mid]
                + k5[1, x - 1, mid] * src[:, x - 1, mid]
                + k5[2, x + 1, mid] * src[:, x + 1, mid]
                + k5[3, x, below] * src[:, x, below]
                + k5[4, x, above] * src[:, x, above]
            )
            return carry

        lax.fori_loop(first, last, body, 0)
        if extra is not None:
            for c in range(4):
                dst[c, X0:X1, Y0:Y1] += extra[c]

    ones = jnp.ones((8, 128), bf16)

    def along(value):
        return lax.dot_general(ones, value, (((1,), (1,)), ((), ())), preferred_element_type=f32)[0:1]

    def looked(state):
        parts = [split(state[c, X0:X1, Y0:Y1].reshape(256, 128)) for c in range(4)]
        halves = [jnp.concatenate([part[k] for part in parts], axis=1) for k in range(2)]
        product = dot(oh[...], jnp.concatenate(halves, axis=0))
        total = None
        for c in range(4):
            term = product[:, c * 128 : (c + 1) * 128] * wc[c]
            total = term if total is None else total + term
        high, low = split(total)
        return along(high) + along(low)

    forward(v0, v1, 2)
    seen = [looked(v1)]
    forward(v1, v2, 1)
    seen.append(looked(v2))
    forward(v2, v3, 0)
    seen.append(looked(v3))

    among(4, not_m, lambda m: value_in(m).wait_recv())
    vi[im] = vo[im]
    scale = glive[...].astype(f32) * gprec[...]
    mask = up == slot_column

    def forcing(step):
        observed = vi[0, step : step + 1] + vi[1, step : step + 1] + vi[2, step : step + 1] + vi[3, step : step + 1]
        misfit = scale * (seen[step] - observed)
        coarse = misfit.astype(bf16).astype(f32)
        fine = misfit - coarse
        high = jnp.where(mask, coarse, 0.0).astype(bf16)
        low = jnp.where(mask, fine, 0.0).astype(bf16)
        product = dot(jnp.concatenate([high, high, low], axis=1), w2[...])
        return [product[:, c * 128 : (c + 1) * 128].reshape(16, 16, 128) for c in range(4)]

    last = forcing(2)
    for c in range(4):
        a3[c, X0:X1, Y0:Y1] = last[c]
    backward(a3, a2, X0 - 1, X1 + 1, forcing(1))
    backward(a2, a1, X0 - 2, X1 + 2, forcing(0))
    backward(a1, v1, X0 - 3, X0, None)
    backward(a1, v1, X1, X1 + 3, None)

    def push_copy(d):
        dx, dy = DIRS[d]
        width = 2 if dx != 0 and dy != 0 else 3
        src = v1.at[:, outer_part(dx, X0, X1, width), outer_part(dy, Y0, Y1, width)]
        at_y = inner_part(-dy, 0, 16, width)
        if dy == 0:
            dst = rx.at[:, inner_part(-dx, 0, 6, width)]
        elif dx == 0:
            dst = ry.at[:, :, at_y]
        else:
            dst = rc.at[:, inner_part(-dx, 0, 4, width), at_y]
        return remote(src, dst, psend.at[d], precv.at[d], ix + dx, iy + dy)

    each(push_copy, start, False, EDGES)
    backward(a1, v1, X0, X1, None)
    each(push_copy, start, False, SIDES)
    each(push_copy, wait_recv, True)
    total = None
    for c in range(4):
        v3[c, X0:X1, Y0:Y1] = v1[c, X0:X1, Y0:Y1] + ry[c]
        v3[c, X0 : X0 + 3, Y0:Y1] += rx[c, 0:3]
        v3[c, X1 - 3 : X1, Y0:Y1] += rx[c, 3:6]
        v3[c, X0 : X0 + 2, Y0:Y1] += rc[c, 0:2]
        v3[c, X1 - 2 : X1, Y0:Y1] += rc[c, 2:4]
        high, low = split(v3[c, X0:X1, Y0:Y1].reshape(256, 128))
        product = dot(selt[:, c * 256 : (c + 1) * 256], jnp.concatenate([high, low], axis=1))
        term = product[:, :128] + product[:, 128:]
        total = term if total is None else total + term
    sums[...] = total.reshape(16, 16, 128)
    strip(lambda t: sums_out(t).start())
    rsums[iy] = sums[iy]
    for c in range(4):
        out_d[c] = dl[c] + v3[c, X0:X1, Y0:Y1]
    strip(lambda t: alpha_out(t).wait_send())
    among(8, lambda q: q != iq, lambda q: obs_out(q).wait_send())
    among(4, not_m, lambda m: index_out(m).wait_send())
    among(4, not_m, lambda m: value_out(m).wait_send())
    each(coef_copy, wait_send, False)
    each(state_copy, wait_send, False)
    each(push_copy, wait_send, False)
    strip(lambda t: sums_in(t).wait_recv())
    result = al[iy] + 0.125 * jnp.sum(rsums[...], axis=0)
    for t in range(4):
        out_a[t] = result[4 * t : 4 * t + 4]
    strip(lambda t: sums_out(t).wait_send())


def on_device(
    delta, alpha, eddy, courant, tile_map, obs_rows,
    gate_beam, gate_index, gate_column, gate_live, obs_weight, obs_precision,
):
    dma = pltpu.SemaphoreType.DMA
    vm = pltpu.VMEM
    frame = vm((4, XB, YB, 128), f32)
    slots = vm((1, 256), jnp.int32)
    anywhere = pl.BlockSpec(memory_space=pl.ANY)
    inside = pl.BlockSpec(memory_space=pltpu.VMEM)
    row = (1, 256)
    grad_delta, grad_alpha = pl.pallas_call(
        kernel,
        out_shape=(vm((4, 16, 16, 128), f32), vm((4, 4, 128), f32)),
        in_specs=[anywhere] * 12,
        out_specs=(inside, inside),
        scratch_shapes=[
            vm((4, 16, 16, 128), f32),
            vm((3, XB, YB, 128), f32),
            vm((5, XB, YB, 128), f32),
            frame, frame, frame, frame,
            frame, frame, frame,
            vm((256, 4, 128), f32),
            vm((4, 256, 128), f32),
            vm((768, 512), bf16),
            vm((16, 16), jnp.int32),
            vm((8, 3, 8, 128), f32),
            vm((4, 2, 256), jnp.int32),
            vm((4, 3, 256), f32),
            vm((4, 3, 256), f32),
            slots, slots,
            vm((1, 256), f32),
            vm((16, 16, 128), f32),
            vm((16, 16, 128), f32),
            vm((16, 16, 128), f32),
            vm((4, 6, 16, 128), f32),
            vm((4, 16, 16, 128), f32),
            vm((4, 4, 16, 128), f32),
            vm((256, 512), bf16),
            vm((1024, 256), bf16),
            vm((256, 1024), bf16),
            dma((12,)),
            dma((16,)), dma((16,)),
            dma((8,)), dma((8,)),
            dma((4,)), dma((4,)),
            dma((4,)), dma((4,)),
            dma((8,)), dma((8,)),
            dma((8,)), dma((8,)),
            dma((8,)), dma((8,)),
            dma((16,)), dma((16,)),
        ],
        compiler_params=pltpu.CompilerParams(
            collective_id=0, has_side_effects=True, vmem_limit_bytes=60 * 1024 * 1024
        ),
    )(
        delta,
        alpha.reshape(16, 128),
        eddy,
        courant,
        tile_map,
        obs_rows.transpose(1, 0, 2),
        gate_beam.reshape(row),
        gate_index.reshape(row),
        gate_column.reshape(row),
        gate_live.reshape(row),
        obs_weight.reshape(256, 4, 128),
        obs_precision.reshape(row),
    )
    return grad_delta, grad_alpha.reshape(1, 4, 4, 128)


def solution(mesh):
    return jax.shard_map(
        on_device,
        mesh=mesh,
        in_specs=(
            P(None, "gx", "gy", None),
            P("gx", "gy", None, None),
            P("gx", "gy", None),
            P(None, "gx", "gy", None),
            P("gx", "gy"),
            P(("gx", "gy"), None, None),
            P("gx", "gy", None),
            P("gx", "gy", None),
            P("gx", "gy", None),
            P("gx", "gy", None),
            P("gx", "gy", None, None, None),
            P("gx", "gy", None),
        ),
        out_specs=(P(None, "gx", "gy", None), P("gx", "gy", None, None)),
        check_vma=False,
    )
```

```python
import jax
import jax.numpy as jnp
from jax import lax
from jax.experimental import pallas as pl
from jax.experimental.pallas import tpu as pltpu
from jax.sharding import PartitionSpec as P

STEPS = 3
MESH = pl.DeviceIdType.MESH
f32 = jnp.float32
bf16 = jnp.bfloat16

X0, X1, XB = 4, 20, 24
Y0, Y1, YB = 8, 24, 32

DIRS = [(1, 0), (-1, 0), (0, 1), (0, -1), (1, 1), (1, -1), (-1, 1), (-1, -1)]


EDGES = (0, 1, 4, 5, 6, 7)
SIDES = (2, 3)


def inner_part(sign, lo, hi, width):
    if sign > 0:
        return pl.ds(hi - width, width)
    if sign < 0:
        return pl.ds(lo, width)
    return pl.ds(lo, hi - lo)


def outer_part(sign, lo, hi, width):
    if sign > 0:
        return pl.ds(hi, width)
    if sign < 0:
        return pl.ds(lo - width, width)
    return pl.ds(lo, hi - lo)


def split(value):
    high = value.astype(bf16)
    low = (value - high.astype(f32)).astype(bf16)
    return high, low


def dot(a, b):
    return jnp.dot(a, b, preferred_element_type=f32)


AT_ONCE = ((), (0,), (0, 1), (0, 1, 2), (0, 1, 2, 3, 5, 6), (0, 1, 2, 3, 4, 6, 7), (0, 1, 2, 3, 4, 5, 7), (0, 1, 2, 3, 5, 6))
THROUGH = ((), (), (), (), ((5, 7),), (), (), ((6, 4),))
ANSWER = (
    ((1, (1,)), (2, (2,)), (7, (7, 6, 5)), (6, (4,)), (3, (3,))),
    ((2, (2,)), (3, (3,)), (7, (7, 6, 5)), (6, (4,))),
    ((3, (3,)), (4, (4, 5, 6)), (5, (7,))),
    ((4, (4, 6)), (5, (5, 7))),
    (), (), (), (),
)


def kernel(
    delta_h, alpha_h, eddy_h, courant_h, tmap_h, obs_h, beam_h, gidx_h, gcol_h, live_h, w_h, prec_h,
    out_d, out_a,
    dl, cf, k5, v0, v1, v2, v3, a1, a2, a3, wv, wc, w2, tm, ob, qi, vo, vi, gcol, glive, gprec,
    al, sums, rsums, rx, ry, rc,
    oh, sel, selt,
    lsem, asend, arecv, osend, orecv, qsend, qrecv, wsend, wrecv,
    csend, crecv, hsend, hrecv, psend, precv, ssend, srecv,
):
    nx = lax.axis_size("gx")
    ny = lax.axis_size("gy")
    nq = nx // 4
    ix = lax.axis_index("gx")
    iy = lax.axis_index("gy")
    iq = ix // 4
    im = ix % 4

    def there(d):
        dx, dy = DIRS[d]
        ok = None
        for sign, at, count in ((dx, ix, nx), (dy, iy, ny)):
            if sign > 0:
                cond = at < count - 1
            elif sign < 0:
                cond = at > 0
            else:
                continue
            ok = cond if ok is None else jnp.logical_and(ok, cond)
        return ok

    def peer(d):
        dx, dy = DIRS[d]
        return {"gx": ix + dx, "gy": iy + dy}

    barrier = pltpu.get_barrier_semaphore()

    def greet(gx, gy):
        pl.semaphore_signal(barrier, inc=1, device_id={"gx": gx, "gy": gy}, device_id_type=MESH)

    def far(table, act):
        for q in range(8):
            if table[q]:

                @pl.when(iq == q)
                def _():
                    for item in table[q]:
                        act(item)

    far([[r for r in range(8) if q in AT_ONCE[r]] for q in range(8)], lambda r: greet(r * 4 + im, iy))

    for t in range(16):

        @pl.when(t != iy)
        def _():
            greet(ix, t)

    greeted = 0
    for q in range(8):
        greeted = greeted + jnp.where(iq == q, len(AT_ONCE[q]), 0)
    expected = (ny - 1) + 3 + greeted
    for d in (0, 1, 4, 5, 6, 7):
        ok = there(d)

        @pl.when(ok)
        def _():
            greet(ix + DIRS[d][0], iy + DIRS[d][1])

        expected = expected + jnp.where(ok, 1, 0)
    for m in range(4):

        @pl.when(m != im)
        def _():
            greet(iq * 4 + m, iy)

    local = [
        pltpu.make_async_copy(alpha_h, al.at[iy], lsem.at[0]),
        pltpu.make_async_copy(obs_h, ob.at[iq], lsem.at[1]),
        pltpu.make_async_copy(eddy_h, cf.at[0, X0:X1, Y0:Y1], lsem.at[2]),
        pltpu.make_async_copy(courant_h, cf.at[pl.ds(1, 2), X0:X1, Y0:Y1], lsem.at[3]),
        pltpu.make_async_copy(beam_h, qi.at[im, pl.ds(0, 1)], lsem.at[4]),
        pltpu.make_async_copy(gidx_h, qi.at[im, pl.ds(1, 1)], lsem.at[5]),
        pltpu.make_async_copy(tmap_h, tm, lsem.at[6]),
        pltpu.make_async_copy(gcol_h, gcol, lsem.at[7]),
        pltpu.make_async_copy(live_h, glive, lsem.at[8]),
        pltpu.make_async_copy(prec_h, gprec, lsem.at[9]),
        pltpu.make_async_copy(w_h, wv, lsem.at[10]),
        pltpu.make_async_copy(delta_h, dl, lsem.at[11]),
    ]
    for copy in local:
        copy.start()

    def remote(src, dst, send, recv, gx, gy):
        return pltpu.make_async_remote_copy(
            src_ref=src,
            dst_ref=dst,
            send_sem=send,
            recv_sem=recv,
            device_id={"gx": gx, "gy": gy},
            device_id_type=MESH,
        )

    def alpha_out(t):
        return remote(al.at[iy], al.at[iy], asend.at[t], arecv.at[iy], ix, t)

    def alpha_in(t):
        return remote(al.at[t], al.at[t], asend.at[t], arecv.at[t], ix, t)

    def obs_out(q):
        return remote(ob.at[iq], ob.at[iq], osend.at[q], orecv.at[iq], q * 4 + im, iy)

    def obs_in(q):
        return remote(ob.at[q], ob.at[q], osend.at[q], orecv.at[q], q * 4 + im, iy)

    def index_out(m):
        return remote(qi.at[im], qi.at[im], qsend.at[m], qrecv.at[im], iq * 4 + m, iy)

    def index_in(m):
        return remote(qi.at[m], qi.at[m], qsend.at[m], qrecv.at[m], iq * 4 + m, iy)

    def value_out(m):
        return remote(vo.at[m], vi.at[im], wsend.at[m], wrecv.at[im], iq * 4 + m, iy)

    def value_in(m):
        return remote(vo.at[m], vi.at[m], wsend.at[m], wrecv.at[m], iq * 4 + m, iy)

    def sums_out(t):
        return remote(sums.at[t], rsums.at[iy], ssend.at[t], srecv.at[iy], ix, t)

    def sums_in(t):
        return remote(sums.at[t], rsums.at[t], ssend.at[t], srecv.at[t], ix, t)

    def among(count, where, act):
        for t in range(count):

            @pl.when(where(t))
            def _():
                act(t)

    ox = (iy // 2) % 4
    others = []
    for dy, dx in ((1, 2), (1, 1), (1, 3), (0, 2), (1, 0), (0, 1), (0, 3), (0, 0)):
        for dc in (1, 0):
            if (dy, dx, dc) != (0, 0, 0):
                ty = (iy // 8 + dy) % 2
                others.append(ty * 8 + ((ox + dx) % 4) * 2 + (iy + dc) % 2)

    def strip(act):
        for t in others:
            act(t)

    def not_m(m):
        return m != im

    local[0].wait()
    local[1].wait()
    pl.semaphore_wait(barrier, expected)
    far(AT_ONCE, lambda q: obs_out(q).start())
    strip(lambda t: alpha_out(t).start())

    def halo_copy(ref, d, width, sends, receives):
        dx, dy = DIRS[d]
        if dx != 0 and dy != 0:
            width = width - 1
        gx, gy = ix + dx, iy + dy
        return remote(
            ref.at[:, inner_part(dx, X0, X1, width), inner_part(dy, Y0, Y1, width)],
            ref.at[:, outer_part(-dx, X0, X1, width), outer_part(-dy, Y0, Y1, width)],
            sends.at[d],
            receives.at[d],
            gx,
            gy,
        )

    def each(make, act, back, those=range(8)):
        for d in those:
            dx, dy = DIRS[d]
            here = DIRS.index((-dx, -dy)) if back else d

            @pl.when(there(here))
            def _():
                act(make(d))

    def start(copy):
        copy.start()

    def wait_send(copy):
        copy.wait_send()

    def wait_recv(copy):
        copy.wait_recv()

    def coef_copy(d):
        return halo_copy(cf, d, 2, csend, crecv)

    def state_copy(d):
        return halo_copy(v0, d, 3, hsend, hrecv)

    local[2].wait()
    local[3].wait()
    each(coef_copy, start, False)
    local[4].wait()
    local[5].wait()
    among(4, not_m, lambda m: index_out(m).start())

    def zero(ref, x, y):
        ref[:, x[0] : x[1], y[0] : y[1]] = jnp.zeros((ref.shape[0], x[1] - x[0], y[1] - y[0], 128), f32)

    def missing(ref, width):
        for d, (dx, dy) in enumerate(DIRS):
            wide = width - 1 if dx != 0 and dy != 0 else width
            spans = []
            for sign, lo, hi in ((dx, X0, X1), (dy, Y0, Y1)):
                spans.append((hi, hi + wide) if sign > 0 else (lo - wide, lo) if sign < 0 else (lo, hi))

            @pl.when(jnp.logical_not(there(d)))
            def _():
                zero(ref, *spans)

    missing(cf, 2)
    missing(v0, 3)
    zero(cf, (0, 2), (0, YB))
    zero(cf, (22, XB), (0, YB))
    zero(cf, (2, 22), (0, 6))
    zero(cf, (2, 22), (26, YB))
    for x in (2, 21):
        zero(cf, (x, x + 1), (6, 8))
        zero(cf, (x, x + 1), (24, 26))
    for x in (3, 20):
        zero(cf, (x, x + 1), (6, 7))
        zero(cf, (x, x + 1), (25, 26))

    local[6].wait()
    lane = lax.broadcasted_iota(jnp.int32, (256, 128), 1)
    row = lax.broadcasted_iota(jnp.int32, (256, 128), 0)
    lanes = lane.astype(f32)
    up = lax.broadcasted_iota(jnp.int32, (256, 256), 0).astype(f32)
    of_row = jnp.where(row // 16 == lane, 1.0, 0.0).astype(bf16)
    tiles = jnp.concatenate(
        [
            jnp.concatenate([tm[...].astype(f32), jnp.zeros((16, 112), f32)], axis=1),
            jnp.zeros((112, 128), f32),
        ],
        axis=0,
    ).astype(bf16)
    picked = jnp.where(row % 16 == lane, dot(of_row, tiles), 0.0).astype(bf16)
    tile_at = dot(picked, jnp.ones((128, 128), bf16)) * 4.0

    def hot(values):
        return jnp.concatenate(
            [jnp.where(values == lanes, 1.0, 0.0), jnp.where(values == lanes + 128.0, 1.0, 0.0)], axis=1
        ).astype(bf16)

    for c in range(4):
        sel[c * 256 : (c + 1) * 256] = hot(tile_at + float(c))
    tile_row = tile_at.T[0:1]
    for c in range(4):
        selt[:, c * 256 : (c + 1) * 256] = jnp.where(up == tile_row + float(c), 1.0, 0.0).astype(bf16)
    for copy in local[7:12]:
        copy.wait()

    slot_column = gcol[0:1].astype(f32)
    at_slot = jnp.where(up == slot_column, 1.0, 0.0).T.astype(bf16)
    oh[:, :256] = at_slot
    oh[:, 256:] = at_slot
    for c in range(4):
        weight = wv[:, c, :]
        high, low = split(weight)
        wc[c] = weight
        w2[0:256, c * 128 : (c + 1) * 128] = high
        w2[256:512, c * 128 : (c + 1) * 128] = low
        w2[512:768, c * 128 : (c + 1) * 128] = high
    rx_rows = ((0, 3), (3, 6))
    for d, x in ((0, rx_rows[1]), (1, rx_rows[0])):

        @pl.when(jnp.logical_not(there(d)))
        def _():
            zero(rx, x, (0, 16))

    zero(ry, (0, 16), (3, 13))
    for d, y in ((2, (13, 16)), (3, (0, 3))):

        @pl.when(jnp.logical_not(there(d)))
        def _():
            zero(ry, (0, 16), y)

    zero(rc, (0, 4), (2, 14))
    for d in (4, 5, 6, 7):
        dx, dy = DIRS[d]

        @pl.when(jnp.logical_not(there(d)))
        def _():
            zero(rc, (2, 4) if dx > 0 else (0, 2), (14, 16) if dy > 0 else (0, 2))

    for ref in (a1, a2, a3):
        zero(ref, (0, X0), (0, YB))
        zero(ref, (X1, XB), (0, YB))
        zero(ref, (X0, X1), (0, Y0))
        zero(ref, (X0, X1), (Y1, YB))

    def through(item):
        obs_in(item[0]).wait_recv()
        obs_out(item[1]).start()

    far(THROUGH, through)

    strip(lambda t: alpha_in(t).wait_recv())
    high, low = split(al[...].reshape(256, 128))
    both = jnp.concatenate([high, low], axis=1)

    def state_rows(x0, x1):
        for c in range(4):
            product = dot(sel[c * 256 + x0 * 16 : c * 256 + x1 * 16], both)
            profile = (product[:, :128] + product[:, 128:]).reshape(x1 - x0, 16, 128)
            v0[c, X0 + x0 : X0 + x1, Y0:Y1] = dl[c, x0:x1] + 0.125 * profile

    state_rows(0, 3)
    state_rows(13, 16)
    each(state_copy, start, False, EDGES)
    state_rows(3, 13)
    each(state_copy, start, False, SIDES)

    def answer(item):
        obs_in(item[0]).wait_recv()
        for q in item[1]:
            obs_out(q).start()

    far([ANSWER[q] if q >= 2 else () for q in range(8)], answer)

    each(coef_copy, wait_recv, True)

    def derive(x, carry):
        e = cf[0, x]
        half_x = 0.5 * cf[1, x]
        half_y = 0.5 * cf[2, x]
        k5[0, x] = 1.0 - 4.0 * e
        k5[1, x] = e - half_x
        k5[2, x] = e + half_x
        k5[3, x] = e - half_y
        k5[4, x] = e + half_y
        return carry

    lax.fori_loop(0, XB, derive, 0, unroll=True)

    far([ANSWER[q] if q < 2 else () for q in range(8)], answer)
    among(4, not_m, lambda m: index_in(m).wait_recv())
    waited = [[t for t, _ in THROUGH[q] + ANSWER[q]] + [q] for q in range(8)]
    far([[r for r in range(8) if r not in waited[q]] for q in range(8)], lambda q: obs_in(q).wait_recv())
    turned = [split(ob[:, step].reshape(64, 128).T) for step in range(STEPS)]
    table = jnp.concatenate([jnp.concatenate(pair, axis=1) for pair in turned], axis=0)
    down64 = lax.broadcasted_iota(jnp.int32, (64, 256), 0)
    down128 = lax.broadcasted_iota(jnp.int32, (128, 256), 0)
    for m in range(4):
        beams = qi[m, 0:1]
        held = jnp.where((beams // 8) % 4 == im, (beams // 32) * 8 + beams % 8, -1)
        at_beam = jnp.where(down64 == held, 1.0, 0.0).astype(bf16)
        found = dot(table, jnp.concatenate([at_beam, at_beam], axis=0))
        at_gate = down128 == qi[m, 1:2]
        for step in range(STEPS):
            both = found[step * 128 : (step + 1) * 128]
            vo[m, step : step + 1] = jnp.sum(jnp.where(at_gate, both, 0.0), axis=0, keepdims=True)

        @pl.when(m != im)
        def _():
            value_out(m).start()


    each(state_copy, wait_recv, True)

    def forward(src, dst, margin):
        y0, rows = (Y0, 16) if margin == 0 else (4, 24)

        def body(x, carry):
            mid = pl.ds(y0, rows)
            dst[:, x, mid] = (
                k5[0, x, mid] * src[:, x, mid]
                + k5[1, x, mid] * src[:, x + 1, mid]
                + k5[2, x, mid] * src[:, x - 1, mid]
                + k5[3, x, mid] * src[:, x, pl.ds(y0 + 1, rows)]
                + k5[4, x, mid] * src[:, x, pl.ds(y0 - 1, rows)]
            )
            return carry

        lax.fori_loop(X0 - margin, X1 + margin, body, 0, unroll=True)

    def backward(src, dst, first, last, extra):
        y0, rows = 4, 24

        def body(x, carry):
            mid = pl.ds(y0, rows)
            below = pl.ds(y0 - 1, rows)
            above = pl.ds(y0 + 1, rows)
            dst[:, x, mid] = (
                k5[0, x, mid] * src[:, x, mid]
                + k5[1, x - 1, mid] * src[:, x - 1, mid]
                + k5[2, x + 1, mid] * src[:, x + 1, mid]
                + k5[3, x, below] * src[:, x, below]
                + k5[4, x, above] * src[:, x, above]
            )
            return carry

        lax.fori_loop(first, last, body, 0, unroll=True)
        if extra is not None:
            for c in range(4):
                dst[c, X0:X1, Y0:Y1] += extra[c]

    ones = jnp.ones((8, 128), bf16)

    def along(value):
        return lax.dot_general(ones, value, (((1,), (1,)), ((), ())), preferred_element_type=f32)[0:1]

    def looked(state):
        parts = [split(state[c, X0:X1, Y0:Y1].reshape(256, 128)) for c in range(4)]
        halves = [jnp.concatenate([part[k] for part in parts], axis=1) for k in range(2)]
        product = dot(oh[...], jnp.concatenate(halves, axis=0))
        total = None
        for c in range(4):
            term = product[:, c * 128 : (c + 1) * 128] * wc[c]
            total = term if total is None else total + term
        high, low = split(total)
        return along(high) + along(low)

    forward(v0, v1, 2)
    seen = [looked(v1)]
    forward(v1, v2, 1)
    seen.append(looked(v2))
    forward(v2, v3, 0)
    seen.append(looked(v3))

    among(4, not_m, lambda m: value_in(m).wait_recv())
    vi[im] = vo[im]
    scale = glive[...].astype(f32) * gprec[...]
    mask = up == slot_column

    def forcing(step):
        observed = vi[0, step : step + 1] + vi[1, step : step + 1] + vi[2, step : step + 1] + vi[3, step : step + 1]
        misfit = scale * (seen[step] - observed)
        coarse = misfit.astype(bf16).astype(f32)
        fine = misfit - coarse
        high = jnp.where(mask, coarse, 0.0).astype(bf16)
        low = jnp.where(mask, fine, 0.0).astype(bf16)
        product = dot(jnp.concatenate([high, high, low], axis=1), w2[...])
        return [product[:, c * 128 : (c + 1) * 128].reshape(16, 16, 128) for c in range(4)]

    last = forcing(2)
    for c in range(4):
        a3[c, X0:X1, Y0:Y1] = last[c]
    backward(a3, a2, X0 - 1, X1 + 1, forcing(1))
    backward(a2, a1, X0 - 2, X1 + 2, forcing(0))
    backward(a1, v1, X0 - 3, X0, None)
    backward(a1, v1, X1, X1 + 3, None)

    def push_copy(d):
        dx, dy = DIRS[d]
        width = 2 if dx != 0 and dy != 0 else 3
        src = v1.at[:, outer_part(dx, X0, X1, width), outer_part(dy, Y0, Y1, width)]
        at_y = inner_part(-dy, 0, 16, width)
        if dy == 0:
            dst = rx.at[:, inner_part(-dx, 0, 6, width)]
        elif dx == 0:
            dst = ry.at[:, :, at_y]
        else:
            dst = rc.at[:, inner_part(-dx, 0, 4, width), at_y]
        return remote(src, dst, psend.at[d], precv.at[d], ix + dx, iy + dy)

    each(push_copy, start, False, EDGES)
    backward(a1, v1, X0, X1, None)
    each(push_copy, start, False, SIDES)
    each(push_copy, wait_recv, True)
    total = None
    for c in range(4):
        v3[c, X0:X1, Y0:Y1] = v1[c, X0:X1, Y0:Y1] + ry[c]
        v3[c, X0 : X0 + 3, Y0:Y1] += rx[c, 0:3]
        v3[c, X1 - 3 : X1, Y0:Y1] += rx[c, 3:6]
        v3[c, X0 : X0 + 2, Y0:Y1] += rc[c, 0:2]
        v3[c, X1 - 2 : X1, Y0:Y1] += rc[c, 2:4]
        high, low = split(v3[c, X0:X1, Y0:Y1].reshape(256, 128))
        product = dot(selt[:, c * 256 : (c + 1) * 256], jnp.concatenate([high, low], axis=1))
        term = product[:, :128] + product[:, 128:]
        total = term if total is None else total + term
    sums[...] = total.reshape(16, 16, 128)
    strip(lambda t: sums_out(t).start())
    rsums[iy] = sums[iy]
    for c in range(4):
        out_d[c] = dl[c] + v3[c, X0:X1, Y0:Y1]
    strip(lambda t: alpha_out(t).wait_send())
    among(8, lambda q: q != iq, lambda q: obs_out(q).wait_send())
    among(4, not_m, lambda m: index_out(m).wait_send())
    among(4, not_m, lambda m: value_out(m).wait_send())
    each(coef_copy, wait_send, False)
    each(state_copy, wait_send, False)
    each(push_copy, wait_send, False)
    strip(lambda t: sums_in(t).wait_recv())
    result = al[iy] + 0.125 * jnp.sum(rsums[...], axis=0)
    for t in range(4):
        out_a[t] = result[4 * t : 4 * t + 4]
    strip(lambda t: sums_out(t).wait_send())


def on_device(
    delta, alpha, eddy, courant, tile_map, obs_rows,
    gate_beam, gate_index, gate_column, gate_live, obs_weight, obs_precision,
):
    dma = pltpu.SemaphoreType.DMA
    vm = pltpu.VMEM
    frame = vm((4, XB, YB, 128), f32)
    slots = vm((1, 256), jnp.int32)
    anywhere = pl.BlockSpec(memory_space=pl.ANY)
    inside = pl.BlockSpec(memory_space=pltpu.VMEM)
    row = (1, 256)
    grad_delta, grad_alpha = pl.pallas_call(
        kernel,
        out_shape=(vm((4, 16, 16, 128), f32), vm((4, 4, 128), f32)),
        in_specs=[anywhere] * 12,
        out_specs=(inside, inside),
        scratch_shapes=[
            vm((4, 16, 16, 128), f32),
            vm((3, XB, YB, 128), f32),
            vm((5, XB, YB, 128), f32),
            frame, frame, frame, frame,
            frame, frame, frame,
            vm((256, 4, 128), f32),
            vm((4, 256, 128), f32),
            vm((768, 512), bf16),
            vm((16, 16), jnp.int32),
            vm((8, 3, 8, 128), f32),
            vm((4, 2, 256), jnp.int32),
            vm((4, 3, 256), f32),
            vm((4, 3, 256), f32),
            slots, slots,
            vm((1, 256), f32),
            vm((16, 16, 128), f32),
            vm((16, 16, 128), f32),
            vm((16, 16, 128), f32),
            vm((4, 6, 16, 128), f32),
            vm((4, 16, 16, 128), f32),
            vm((4, 4, 16, 128), f32),
            vm((256, 512), bf16),
            vm((1024, 256), bf16),
            vm((256, 1024), bf16),
            dma((12,)),
            dma((16,)), dma((16,)),
            dma((8,)), dma((8,)),
            dma((4,)), dma((4,)),
            dma((4,)), dma((4,)),
            dma((8,)), dma((8,)),
            dma((8,)), dma((8,)),
            dma((8,)), dma((8,)),
            dma((16,)), dma((16,)),
        ],
        compiler_params=pltpu.CompilerParams(
            collective_id=0, has_side_effects=True, vmem_limit_bytes=60 * 1024 * 1024
        ),
    )(
        delta,
        alpha.reshape(16, 128),
        eddy,
        courant,
        tile_map,
        obs_rows.transpose(1, 0, 2),
        gate_beam.reshape(row),
        gate_index.reshape(row),
        gate_column.reshape(row),
        gate_live.reshape(row),
        obs_weight.reshape(256, 4, 128),
        obs_precision.reshape(row),
    )
    return grad_delta, grad_alpha.reshape(1, 4, 4, 128)


def solution(mesh):
    return jax.shard_map(
        on_device,
        mesh=mesh,
        in_specs=(
            P(None, "gx", "gy", None),
            P("gx", "gy", None, None),
            P("gx", "gy", None),
            P(None, "gx", "gy", None),
            P("gx", "gy"),
            P(("gx", "gy"), None, None),
            P("gx", "gy", None),
            P("gx", "gy", None),
            P("gx", "gy", None),
            P("gx", "gy", None),
            P("gx", "gy", None, None, None),
            P("gx", "gy", None),
        ),
        out_specs=(P(None, "gx", "gy", None), P("gx", "gy", None, None)),
        check_vma=False,
    )
```

```python
import jax
import jax.numpy as jnp
from jax import lax
from jax.experimental import pallas as pl
from jax.experimental.pallas import tpu as pltpu
from jax.sharding import PartitionSpec as P

STEPS = 3
MESH = pl.DeviceIdType.MESH
f32 = jnp.float32
bf16 = jnp.bfloat16

X0, X1, XB = 4, 20, 24
Y0, Y1, YB = 8, 24, 32

DIRS = [(1, 0), (-1, 0), (0, 1), (0, -1), (1, 1), (1, -1), (-1, 1), (-1, -1)]


EDGES = (0, 1, 4, 5, 6, 7)
SIDES = (2, 3)


def inner_part(sign, lo, hi, width):
    if sign > 0:
        return pl.ds(hi - width, width)
    if sign < 0:
        return pl.ds(lo, width)
    return pl.ds(lo, hi - lo)


def outer_part(sign, lo, hi, width):
    if sign > 0:
        return pl.ds(hi, width)
    if sign < 0:
        return pl.ds(lo - width, width)
    return pl.ds(lo, hi - lo)


def split(value):
    high = value.astype(bf16)
    low = (value - high.astype(f32)).astype(bf16)
    return high, low


def dot(a, b):
    return jnp.dot(a, b, preferred_element_type=f32)


AT_ONCE = ((), (0,), (0, 1), (0, 1, 2), (0, 1, 2, 3, 5, 6, 7), (0, 1, 2, 3, 4, 6, 7), (0, 1, 2, 3, 4, 5, 7), (0, 1, 2, 3, 5, 6))
THROUGH = ((), (), (), (), (), (), (), ((6, 4),))
ANSWER = (
    ((1, (1,)), (2, (2,)), (7, (7, 6, 5)), (6, (4,)), (3, (3,))),
    ((2, (2,)), (3, (3,)), (7, (7, 6, 5)), (6, (4,))),
    ((3, (3,)), (4, (4, 5, 6, 7))),
    ((4, (4, 5, 6, 7)),),
    (), (), (), (),
)


def kernel(
    delta_h, alpha_h, eddy_h, courant_h, tmap_h, obs_h, beam_h, gidx_h, gcol_h, live_h, w_h, prec_h,
    out_d, out_a,
    dl, cf, k5, v0, v1, v2, v3, a1, a2, a3, wv, wc, w2, tm, ob, qi, vo, vi, gcol, glive, gprec,
    al, sums, rsums, rx, ry, rc,
    oh, sel, selt,
    lsem, asend, arecv, osend, orecv, qsend, qrecv, wsend, wrecv,
    csend, crecv, hsend, hrecv, psend, precv, ssend, srecv,
):
    nx = lax.axis_size("gx")
    ny = lax.axis_size("gy")
    nq = nx // 4
    ix = lax.axis_index("gx")
    iy = lax.axis_index("gy")
    iq = ix // 4
    im = ix % 4

    def there(d):
        dx, dy = DIRS[d]
        ok = None
        for sign, at, count in ((dx, ix, nx), (dy, iy, ny)):
            if sign > 0:
                cond = at < count - 1
            elif sign < 0:
                cond = at > 0
            else:
                continue
            ok = cond if ok is None else jnp.logical_and(ok, cond)
        return ok

    def peer(d):
        dx, dy = DIRS[d]
        return {"gx": ix + dx, "gy": iy + dy}

    barrier = pltpu.get_barrier_semaphore()

    def greet(gx, gy):
        pl.semaphore_signal(barrier, inc=1, device_id={"gx": gx, "gy": gy}, device_id_type=MESH)

    def far(table, act):
        for q in range(8):
            if table[q]:

                @pl.when(iq == q)
                def _():
                    for item in table[q]:
                        act(item)

    far([[r for r in range(8) if q in AT_ONCE[r]] for q in range(8)], lambda r: greet(r * 4 + im, iy))

    for t in range(16):

        @pl.when(t != iy)
        def _():
            greet(ix, t)

    greeted = 0
    for q in range(8):
        greeted = greeted + jnp.where(iq == q, len(AT_ONCE[q]), 0)
    expected = (ny - 1) + 3 + greeted
    for d in (0, 1, 4, 5, 6, 7):
        ok = there(d)

        @pl.when(ok)
        def _():
            greet(ix + DIRS[d][0], iy + DIRS[d][1])

        expected = expected + jnp.where(ok, 1, 0)
    for m in range(4):

        @pl.when(m != im)
        def _():
            greet(iq * 4 + m, iy)

    local = [
        pltpu.make_async_copy(alpha_h, al.at[iy], lsem.at[0]),
        pltpu.make_async_copy(obs_h, ob.at[iq], lsem.at[1]),
        pltpu.make_async_copy(eddy_h, cf.at[0, X0:X1, Y0:Y1], lsem.at[2]),
        pltpu.make_async_copy(courant_h, cf.at[pl.ds(1, 2), X0:X1, Y0:Y1], lsem.at[3]),
        pltpu.make_async_copy(beam_h, qi.at[im, pl.ds(0, 1)], lsem.at[4]),
        pltpu.make_async_copy(gidx_h, qi.at[im, pl.ds(1, 1)], lsem.at[5]),
        pltpu.make_async_copy(tmap_h, tm, lsem.at[6]),
        pltpu.make_async_copy(gcol_h, gcol, lsem.at[7]),
        pltpu.make_async_copy(live_h, glive, lsem.at[8]),
        pltpu.make_async_copy(prec_h, gprec, lsem.at[9]),
        pltpu.make_async_copy(w_h, wv, lsem.at[10]),
        pltpu.make_async_copy(delta_h, dl, lsem.at[11]),
    ]
    for copy in local:
        copy.start()

    def remote(src, dst, send, recv, gx, gy):
        return pltpu.make_async_remote_copy(
            src_ref=src,
            dst_ref=dst,
            send_sem=send,
            recv_sem=recv,
            device_id={"gx": gx, "gy": gy},
            device_id_type=MESH,
        )

    def alpha_out(t):
        return remote(al.at[iy], al.at[iy], asend.at[t], arecv.at[iy], ix, t)

    def alpha_in(t):
        return remote(al.at[t], al.at[t], asend.at[t], arecv.at[t], ix, t)

    def obs_out(q):
        return remote(ob.at[iq], ob.at[iq], osend.at[q], orecv.at[iq], q * 4 + im, iy)

    def obs_in(q):
        return remote(ob.at[q], ob.at[q], osend.at[q], orecv.at[q], q * 4 + im, iy)

    def index_out(m):
        return remote(qi.at[im], qi.at[im], qsend.at[m], qrecv.at[im], iq * 4 + m, iy)

    def index_in(m):
        return remote(qi.at[m], qi.at[m], qsend.at[m], qrecv.at[m], iq * 4 + m, iy)

    def value_out(m):
        return remote(vo.at[m], vi.at[im], wsend.at[m], wrecv.at[im], iq * 4 + m, iy)

    def value_in(m):
        return remote(vo.at[m], vi.at[m], wsend.at[m], wrecv.at[m], iq * 4 + m, iy)

    def sums_out(t):
        return remote(sums.at[t], rsums.at[iy], ssend.at[t], srecv.at[iy], ix, t)

    def sums_in(t):
        return remote(sums.at[t], rsums.at[t], ssend.at[t], srecv.at[t], ix, t)

    def among(count, where, act):
        for t in range(count):

            @pl.when(where(t))
            def _():
                act(t)

    ox = (iy // 2) % 4
    others = []
    for dy, dx in ((1, 2), (1, 1), (1, 3), (0, 2), (1, 0), (0, 1), (0, 3), (0, 0)):
        for dc in (1, 0):
            if (dy, dx, dc) != (0, 0, 0):
                ty = (iy // 8 + dy) % 2
                others.append(ty * 8 + ((ox + dx) % 4) * 2 + (iy + dc) % 2)

    def strip(act):
        for t in others:
            act(t)

    def not_m(m):
        return m != im

    local[0].wait()
    local[1].wait()
    pl.semaphore_wait(barrier, expected)
    far(AT_ONCE, lambda q: obs_out(q).start())
    strip(lambda t: alpha_out(t).start())

    def halo_copy(ref, d, width, sends, receives):
        dx, dy = DIRS[d]
        if dx != 0 and dy != 0:
            width = width - 1
        gx, gy = ix + dx, iy + dy
        return remote(
            ref.at[:, inner_part(dx, X0, X1, width), inner_part(dy, Y0, Y1, width)],
            ref.at[:, outer_part(-dx, X0, X1, width), outer_part(-dy, Y0, Y1, width)],
            sends.at[d],
            receives.at[d],
            gx,
            gy,
        )

    def each(make, act, back, those=range(8)):
        for d in those:
            dx, dy = DIRS[d]
            here = DIRS.index((-dx, -dy)) if back else d

            @pl.when(there(here))
            def _():
                act(make(d))

    def start(copy):
        copy.start()

    def wait_send(copy):
        copy.wait_send()

    def wait_recv(copy):
        copy.wait_recv()

    def coef_copy(d):
        return halo_copy(cf, d, 2, csend, crecv)

    def state_copy(d):
        return halo_copy(v0, d, 3, hsend, hrecv)

    local[2].wait()
    local[3].wait()
    each(coef_copy, start, False)
    local[4].wait()
    local[5].wait()
    among(4, not_m, lambda m: index_out(m).start())

    def zero(ref, x, y):
        ref[:, x[0] : x[1], y[0] : y[1]] = jnp.zeros((ref.shape[0], x[1] - x[0], y[1] - y[0], 128), f32)

    def missing(ref, width):
        for d, (dx, dy) in enumerate(DIRS):
            wide = width - 1 if dx != 0 and dy != 0 else width
            spans = []
            for sign, lo, hi in ((dx, X0, X1), (dy, Y0, Y1)):
                spans.append((hi, hi + wide) if sign > 0 else (lo - wide, lo) if sign < 0 else (lo, hi))

            @pl.when(jnp.logical_not(there(d)))
            def _():
                zero(ref, *spans)

    missing(cf, 2)
    missing(v0, 3)
    zero(cf, (0, 2), (0, YB))
    zero(cf, (22, XB), (0, YB))
    zero(cf, (2, 22), (0, 6))
    zero(cf, (2, 22), (26, YB))
    for x in (2, 21):
        zero(cf, (x, x + 1), (6, 8))
        zero(cf, (x, x + 1), (24, 26))
    for x in (3, 20):
        zero(cf, (x, x + 1), (6, 7))
        zero(cf, (x, x + 1), (25, 26))

    local[6].wait()
    lane = lax.broadcasted_iota(jnp.int32, (256, 128), 1)
    row = lax.broadcasted_iota(jnp.int32, (256, 128), 0)
    lanes = lane.astype(f32)
    up = lax.broadcasted_iota(jnp.int32, (256, 256), 0).astype(f32)
    of_row = jnp.where(row // 16 == lane, 1.0, 0.0).astype(bf16)
    tiles = jnp.concatenate(
        [
            jnp.concatenate([tm[...].astype(f32), jnp.zeros((16, 112), f32)], axis=1),
            jnp.zeros((112, 128), f32),
        ],
        axis=0,
    ).astype(bf16)
    picked = jnp.where(row % 16 == lane, dot(of_row, tiles), 0.0).astype(bf16)
    tile_at = dot(picked, jnp.ones((128, 128), bf16)) * 4.0

    def hot(values):
        return jnp.concatenate(
            [jnp.where(values == lanes, 1.0, 0.0), jnp.where(values == lanes + 128.0, 1.0, 0.0)], axis=1
        ).astype(bf16)

    for c in range(4):
        sel[c * 256 : (c + 1) * 256] = hot(tile_at + float(c))
    tile_row = tile_at.T[0:1]
    for c in range(4):
        selt[:, c * 256 : (c + 1) * 256] = jnp.where(up == tile_row + float(c), 1.0, 0.0).astype(bf16)
    for copy in local[7:12]:
        copy.wait()

    slot_column = gcol[0:1].astype(f32)
    at_slot = jnp.where(up == slot_column, 1.0, 0.0).T.astype(bf16)
    oh[:, :256] = at_slot
    oh[:, 256:] = at_slot
    for c in range(4):
        weight = wv[:, c, :]
        high, low = split(weight)
        wc[c] = weight
        w2[0:256, c * 128 : (c + 1) * 128] = high
        w2[256:512, c * 128 : (c + 1) * 128] = low
        w2[512:768, c * 128 : (c + 1) * 128] = high
    rx_rows = ((0, 3), (3, 6))
    for d, x in ((0, rx_rows[1]), (1, rx_rows[0])):

        @pl.when(jnp.logical_not(there(d)))
        def _():
            zero(rx, x, (0, 16))

    zero(ry, (0, 16), (3, 13))
    for d, y in ((2, (13, 16)), (3, (0, 3))):

        @pl.when(jnp.logical_not(there(d)))
        def _():
            zero(ry, (0, 16), y)

    zero(rc, (0, 4), (2, 14))
    for d in (4, 5, 6, 7):
        dx, dy = DIRS[d]

        @pl.when(jnp.logical_not(there(d)))
        def _():
            zero(rc, (2, 4) if dx > 0 else (0, 2), (14, 16) if dy > 0 else (0, 2))

    for ref in (a1, a2, a3):
        zero(ref, (0, X0), (0, YB))
        zero(ref, (X1, XB), (0, YB))
        zero(ref, (X0, X1), (0, Y0))
        zero(ref, (X0, X1), (Y1, YB))

    def through(item):
        obs_in(item[0]).wait_recv()
        obs_out(item[1]).start()

    far(THROUGH, through)

    strip(lambda t: alpha_in(t).wait_recv())
    high, low = split(al[...].reshape(256, 128))
    both = jnp.concatenate([high, low], axis=1)

    def state_rows(x0, x1):
        for c in range(4):
            product = dot(sel[c * 256 + x0 * 16 : c * 256 + x1 * 16], both)
            profile = (product[:, :128] + product[:, 128:]).reshape(x1 - x0, 16, 128)
            v0[c, X0 + x0 : X0 + x1, Y0:Y1] = dl[c, x0:x1] + 0.125 * profile

    state_rows(0, 3)
    state_rows(13, 16)
    each(state_copy, start, False, EDGES)
    state_rows(3, 13)
    each(state_copy, start, False, SIDES)

    def answer(item):
        obs_in(item[0]).wait_recv()
        for q in item[1]:
            obs_out(q).start()

    far([ANSWER[q] if q >= 2 else () for q in range(8)], answer)

    each(coef_copy, wait_recv, True)

    def derive(x, carry):
        e = cf[0, x]
        half_x = 0.5 * cf[1, x]
        half_y = 0.5 * cf[2, x]
        k5[0, x] = 1.0 - 4.0 * e
        k5[1, x] = e - half_x
        k5[2, x] = e + half_x
        k5[3, x] = e - half_y
        k5[4, x] = e + half_y
        return carry

    lax.fori_loop(0, XB, derive, 0, unroll=True)

    far([ANSWER[q] if q < 2 else () for q in range(8)], answer)
    among(4, not_m, lambda m: index_in(m).wait_recv())
    waited = [[t for t, _ in THROUGH[q] + ANSWER[q]] + [q] for q in range(8)]
    far([[r for r in range(8) if r not in waited[q]] for q in range(8)], lambda q: obs_in(q).wait_recv())
    turned = [split(ob[:, step].reshape(64, 128).T) for step in range(STEPS)]
    table = jnp.concatenate([jnp.concatenate(pair, axis=1) for pair in turned], axis=0)
    down64 = lax.broadcasted_iota(jnp.int32, (64, 256), 0)
    down128 = lax.broadcasted_iota(jnp.int32, (128, 256), 0)
    for m in range(4):
        beams = qi[m, 0:1]
        held = jnp.where((beams // 8) % 4 == im, (beams // 32) * 8 + beams % 8, -1)
        at_beam = jnp.where(down64 == held, 1.0, 0.0).astype(bf16)
        found = dot(table, jnp.concatenate([at_beam, at_beam], axis=0))
        at_gate = down128 == qi[m, 1:2]
        for step in range(STEPS):
            both = found[step * 128 : (step + 1) * 128]
            vo[m, step : step + 1] = jnp.sum(jnp.where(at_gate, both, 0.0), axis=0, keepdims=True)

        @pl.when(m != im)
        def _():
            value_out(m).start()


    each(state_copy, wait_recv, True)

    def forward(src, dst, margin):
        y0, rows = (Y0, 16) if margin == 0 else (4, 24)

        def body(x, carry):
            mid = pl.ds(y0, rows)
            dst[:, x, mid] = (
                k5[0, x, mid] * src[:, x, mid]
                + k5[1, x, mid] * src[:, x + 1, mid]
                + k5[2, x, mid] * src[:, x - 1, mid]
                + k5[3, x, mid] * src[:, x, pl.ds(y0 + 1, rows)]
                + k5[4, x, mid] * src[:, x, pl.ds(y0 - 1, rows)]
            )
            return carry

        lax.fori_loop(X0 - margin, X1 + margin, body, 0, unroll=True)

    def backward(src, dst, first, last, extra):
        y0, rows = 4, 24

        def body(x, carry):
            mid = pl.ds(y0, rows)
            below = pl.ds(y0 - 1, rows)
            above = pl.ds(y0 + 1, rows)
            dst[:, x, mid] = (
                k5[0, x, mid] * src[:, x, mid]
                + k5[1, x - 1, mid] * src[:, x - 1, mid]
                + k5[2, x + 1, mid] * src[:, x + 1, mid]
                + k5[3, x, below] * src[:, x, below]
                + k5[4, x, above] * src[:, x, above]
            )
            return carry

        lax.fori_loop(first, last, body, 0, unroll=True)
        if extra is not None:
            for c in range(4):
                dst[c, X0:X1, Y0:Y1] += extra[c]

    ones = jnp.ones((8, 128), bf16)

    def along(value):
        return lax.dot_general(ones, value, (((1,), (1,)), ((), ())), preferred_element_type=f32)[0:1]

    def looked(state):
        parts = [split(state[c, X0:X1, Y0:Y1].reshape(256, 128)) for c in range(4)]
        halves = [jnp.concatenate([part[k] for part in parts], axis=1) for k in range(2)]
        product = dot(oh[...], jnp.concatenate(halves, axis=0))
        total = None
        for c in range(4):
            term = product[:, c * 128 : (c + 1) * 128] * wc[c]
            total = term if total is None else total + term
        high, low = split(total)
        return along(high) + along(low)

    forward(v0, v1, 2)
    seen = [looked(v1)]
    forward(v1, v2, 1)
    seen.append(looked(v2))
    forward(v2, v3, 0)
    seen.append(looked(v3))

    among(4, not_m, lambda m: value_in(m).wait_recv())
    vi[im] = vo[im]
    scale = glive[...].astype(f32) * gprec[...]
    mask = up == slot_column

    def forcing(step):
        observed = vi[0, step : step + 1] + vi[1, step : step + 1] + vi[2, step : step + 1] + vi[3, step : step + 1]
        misfit = scale * (seen[step] - observed)
        coarse = misfit.astype(bf16).astype(f32)
        fine = misfit - coarse
        high = jnp.where(mask, coarse, 0.0).astype(bf16)
        low = jnp.where(mask, fine, 0.0).astype(bf16)
        product = dot(jnp.concatenate([high, high, low], axis=1), w2[...])
        return [product[:, c * 128 : (c + 1) * 128].reshape(16, 16, 128) for c in range(4)]

    last = forcing(2)
    for c in range(4):
        a3[c, X0:X1, Y0:Y1] = last[c]
    backward(a3, a2, X0 - 1, X1 + 1, forcing(1))
    backward(a2, a1, X0 - 2, X1 + 2, forcing(0))
    backward(a1, v1, X0 - 3, X0, None)
    backward(a1, v1, X1, X1 + 3, None)

    def push_copy(d):
        dx, dy = DIRS[d]
        width = 2 if dx != 0 and dy != 0 else 3
        src = v1.at[:, outer_part(dx, X0, X1, width), outer_part(dy, Y0, Y1, width)]
        at_y = inner_part(-dy, 0, 16, width)
        if dy == 0:
            dst = rx.at[:, inner_part(-dx, 0, 6, width)]
        elif dx == 0:
            dst = ry.at[:, :, at_y]
        else:
            dst = rc.at[:, inner_part(-dx, 0, 4, width), at_y]
        return remote(src, dst, psend.at[d], precv.at[d], ix + dx, iy + dy)

    each(push_copy, start, False, EDGES)
    backward(a1, v1, X0, X1, None)
    each(push_copy, start, False, SIDES)
    each(push_copy, wait_recv, True)
    total = None
    for c in range(4):
        own = v1[c, X0:X1, Y0:Y1] + ry[c]
        whole = jnp.concatenate(
            [
                own[0:2] + rx[c, 0:2] + rc[c, 0:2],
                own[2:3] + rx[c, 2:3],
                own[3:13],
                own[13:14] + rx[c, 3:4],
                own[14:16] + rx[c, 4:6] + rc[c, 2:4],
            ],
            axis=0,
        )
        v3[c, X0:X1, Y0:Y1] = whole
        high, low = split(whole.reshape(256, 128))
        product = dot(selt[:, c * 256 : (c + 1) * 256], jnp.concatenate([high, low], axis=1))
        term = product[:, :128] + product[:, 128:]
        total = term if total is None else total + term
    sums[...] = total.reshape(16, 16, 128)
    strip(lambda t: sums_out(t).start())
    rsums[iy] = sums[iy]
    for c in range(4):
        out_d[c] = dl[c] + v3[c, X0:X1, Y0:Y1]
    strip(lambda t: alpha_out(t).wait_send())
    among(8, lambda q: q != iq, lambda q: obs_out(q).wait_send())
    among(4, not_m, lambda m: index_out(m).wait_send())
    among(4, not_m, lambda m: value_out(m).wait_send())
    each(coef_copy, wait_send, False)
    each(state_copy, wait_send, False)
    each(push_copy, wait_send, False)
    strip(lambda t: sums_in(t).wait_recv())
    result = al[iy] + 0.125 * jnp.sum(rsums[...], axis=0)
    for t in range(4):
        out_a[t] = result[4 * t : 4 * t + 4]
    strip(lambda t: sums_out(t).wait_send())


def on_device(
    delta, alpha, eddy, courant, tile_map, obs_rows,
    gate_beam, gate_index, gate_column, gate_live, obs_weight, obs_precision,
):
    dma = pltpu.SemaphoreType.DMA
    vm = pltpu.VMEM
    frame = vm((4, XB, YB, 128), f32)
    slots = vm((1, 256), jnp.int32)
    anywhere = pl.BlockSpec(memory_space=pl.ANY)
    inside = pl.BlockSpec(memory_space=pltpu.VMEM)
    row = (1, 256)
    grad_delta, grad_alpha = pl.pallas_call(
        kernel,
        out_shape=(vm((4, 16, 16, 128), f32), vm((4, 4, 128), f32)),
        in_specs=[anywhere] * 12,
        out_specs=(inside, inside),
        scratch_shapes=[
            vm((4, 16, 16, 128), f32),
            vm((3, XB, YB, 128), f32),
            vm((5, XB, YB, 128), f32),
            frame, frame, frame, frame,
            frame, frame, frame,
            vm((256, 4, 128), f32),
            vm((4, 256, 128), f32),
            vm((768, 512), bf16),
            vm((16, 16), jnp.int32),
            vm((8, 3, 8, 128), f32),
            vm((4, 2, 256), jnp.int32),
            vm((4, 3, 256), f32),
            vm((4, 3, 256), f32),
            slots, slots,
            vm((1, 256), f32),
            vm((16, 16, 128), f32),
            vm((16, 16, 128), f32),
            vm((16, 16, 128), f32),
            vm((4, 6, 16, 128), f32),
            vm((4, 16, 16, 128), f32),
            vm((4, 4, 16, 128), f32),
            vm((256, 512), bf16),
            vm((1024, 256), bf16),
            vm((256, 1024), bf16),
            dma((12,)),
            dma((16,)), dma((16,)),
            dma((8,)), dma((8,)),
            dma((4,)), dma((4,)),
            dma((4,)), dma((4,)),
            dma((8,)), dma((8,)),
            dma((8,)), dma((8,)),
            dma((8,)), dma((8,)),
            dma((16,)), dma((16,)),
        ],
        compiler_params=pltpu.CompilerParams(
            collective_id=0, has_side_effects=True, vmem_limit_bytes=60 * 1024 * 1024
        ),
    )(
        delta,
        alpha.reshape(16, 128),
        eddy,
        courant,
        tile_map,
        obs_rows.transpose(1, 0, 2),
        gate_beam.reshape(row),
        gate_index.reshape(row),
        gate_column.reshape(row),
        gate_live.reshape(row),
        obs_weight.reshape(256, 4, 128),
        obs_precision.reshape(row),
    )
    return grad_delta, grad_alpha.reshape(1, 4, 4, 128)


def solution(mesh):
    return jax.shard_map(
        on_device,
        mesh=mesh,
        in_specs=(
            P(None, "gx", "gy", None),
            P("gx", "gy", None, None),
            P("gx", "gy", None),
            P(None, "gx", "gy", None),
            P("gx", "gy"),
            P(("gx", "gy"), None, None),
            P("gx", "gy", None),
            P("gx", "gy", None),
            P("gx", "gy", None),
            P("gx", "gy", None),
            P("gx", "gy", None, None, None),
            P("gx", "gy", None),
        ),
        out_specs=(P(None, "gx", "gy", None), P("gx", "gy", None, None)),
        check_vma=False,
    )
```
